32 devices in a mesh: row: 4 (over y, x), col: 8 (over z, core).
Axes of the slice: x: 2, y: 2, z: 4, core: 2. Of those that a mesh axis runs over, the one named last changes fastest.
Arguments:
- history: bfloat16 [2, 4096, 4096], P(None, 'row', 'col'), may hold values from -2 to 2, as said below
- start_strip: float32 [2, 2048, 4096], P(None, 'col', 'row'), may hold values from -6 to 6
- coupling: float32 [32], replicated, may hold values from 0.5 to 1.5
- dyson_inverse: float32 [2, 2, 64, 64], replicated, may hold values from -3 to 3, as said below
Outputs:
- earlier: float32 [2, 2048, 4096], P(None, None, 'col')
- later: float32 [2, 2048, 4096], P(None, 'col', 'row')
The draws below stay inside these ranges and needn't reach their ends.
Inputs may be any that keep to these rules, and one draw needn't show every extreme that they name: history is anti-Hermitian: its element at row (s, a), column (t, b) is minus the complex conjugate of its element at row (t, b), column (s, a). `dyson_inverse`: each group's inverse is lower triangular in time.
All inputs are finite; a program needn't handle non-finite values.
Results may differ from the reference program's by a relative error of at most 0.0043.
Values may be sent and summed in bfloat16 or wider, within the bound.
A program may use at most 192 MiB of HBM per device.

```python
import math
import jax
import jax.numpy as jnp
from jax import lax

NO = 32
C = 64
NT = 128


def draw_history(key, part):
    width = NT * NO
    key_real = jax.random.fold_in(key, 11)
    key_imag = jax.random.fold_in(key, 12)
    noise_real = jax.random.normal(key_real, (width, width), jnp.float32) * width ** (-0.5)
    noise_imag = jax.random.normal(key_imag, (width, width), jnp.float32) * width ** (-0.5)
    real_part = (noise_real - noise_real.T) * 0.5
    imag_part = (noise_imag + noise_imag.T) * 0.5
    return jnp.stack([real_part, imag_part]).astype(jnp.bfloat16)


def draw_dyson_inverse(key, part):
    key_real = jax.random.fold_in(key, 21)
    key_imag = jax.random.fold_in(key, 22)
    lower = jnp.tril(jnp.ones((C, C), jnp.float32))
    noise_real = jax.random.normal(key_real, (2, C, C), jnp.float32) * (0.5 * C ** (-0.5))
    noise_imag = jax.random.normal(key_imag, (2, C, C), jnp.float32) * (0.5 * C ** (-0.5))
    real_part = jnp.eye(C, dtype=jnp.float32)[None] + noise_real * lower[None]
    imag_part = noise_imag * lower[None]
    return jnp.stack([real_part, imag_part], axis=1)


def levels(own_key, dims, shards, least, high):
    level = 1.0
    for axis_at, blocks in shards:
        steps = jax.random.uniform(jax.random.fold_in(jax.random.fold_in(own_key, 6), axis_at), (blocks,), jnp.float32, least / len(shards), high / len(shards))
        level = level * jnp.repeat(jnp.exp(steps), dims[axis_at] // blocks).reshape((-1,) + (1,) * (len(dims) - 1 - axis_at))
    return level


def normal_values(own_key, dims, scale, limit, shards=(), kind=jnp.bfloat16):
    loudness = levels(own_key, dims, shards, -0.22, 0.18) if shards else 1.0
    array = jax.random.normal(own_key, dims, jnp.float32) * scale * loudness
    return jnp.minimum(jnp.maximum(array, -limit), limit).astype(kind)


def setup_inputs(seed: int = 0) -> dict:
    splits = jax.random.split(jax.random.key(seed), 5)
    history = draw_history(jax.random.fold_in(splits[4], 71), 0)
    start_strip = normal_values(splits[1], (2, C * NO, NT * NO), 1.0, 6.0, ((1, 8), (2, 4)), jnp.float32)
    coupling = jnp.clip(jnp.exp(jax.random.uniform(splits[2], (NO,), jnp.float32, math.log(0.5), math.log(1.5))), 0.5, 1.5)
    dyson_inverse = draw_dyson_inverse(jax.random.fold_in(splits[4], 71), 0)
    return {"history": history, "start_strip": start_strip, "coupling": coupling, "dyson_inverse": dyson_inverse}


TIME_STEP = 0.15


def complex_product(first_pair, second_pair):
    real_out = jnp.dot(first_pair[0], second_pair[0], precision=lax.Precision.HIGHEST, preferred_element_type=jnp.float32) - jnp.dot(first_pair[1], second_pair[1], precision=lax.Precision.HIGHEST, preferred_element_type=jnp.float32)
    imag_out = jnp.dot(first_pair[0], second_pair[1], precision=lax.Precision.HIGHEST, preferred_element_type=jnp.float32) + jnp.dot(first_pair[1], second_pair[0], precision=lax.Precision.HIGHEST, preferred_element_type=jnp.float32)
    return jnp.stack([real_out, imag_out])


def self_energy(green, row_weight, col_weight):
    magnitude = green[0] * green[0] + green[1] * green[1]
    factor = -(row_weight[:, None] * col_weight[None, :]) * magnitude
    return green * factor[None]


def dyson_apply(inverse, source):
    group_len = inverse.shape[1]
    flat_width = source.shape[1] * source.shape[2] // group_len
    flat = source.reshape(2, group_len, flat_width)
    real_out = jnp.dot(inverse[0], flat[0], precision=lax.Precision.HIGHEST, preferred_element_type=jnp.float32) - jnp.dot(inverse[1], flat[1], precision=lax.Precision.HIGHEST, preferred_element_type=jnp.float32)
    imag_out = jnp.dot(inverse[0], flat[1], precision=lax.Precision.HIGHEST, preferred_element_type=jnp.float32) + jnp.dot(inverse[1], flat[0], precision=lax.Precision.HIGHEST, preferred_element_type=jnp.float32)
    return jnp.stack([real_out, imag_out]).reshape(source.shape)


def reference(history, start_strip, coupling, dyson_inverse):
    hist_wide = history.astype(jnp.float32)
    row_weight = jnp.tile(coupling, C)
    col_weight = jnp.tile(coupling, NT)
    sigma_first = self_energy(start_strip, row_weight, col_weight).astype(jnp.bfloat16)
    sigma_first = lax.optimization_barrier(sigma_first).astype(jnp.float32)
    earlier = dyson_apply(dyson_inverse[0], TIME_STEP * complex_product(sigma_first, hist_wide))
    sigma_second = self_energy(earlier, row_weight, col_weight).astype(jnp.bfloat16)
    sigma_second = lax.optimization_barrier(sigma_second).astype(jnp.float32)
    later = dyson_apply(dyson_inverse[1], TIME_STEP * complex_product(sigma_second, hist_wide))
    return earlier, later
```

```python
import functools

import jax
import jax.numpy as jnp
from jax import lax
from jax.experimental import pallas as pl
from jax.experimental.pallas import tpu as pltpu
from jax.sharding import PartitionSpec as P

TIME_STEP = 0.15


def complex_product(first_pair, second_pair):
    real_out = jnp.dot(first_pair[0], second_pair[0], preferred_element_type=jnp.float32) - jnp.dot(
        first_pair[1], second_pair[1], preferred_element_type=jnp.float32
    )
    imag_out = jnp.dot(first_pair[0], second_pair[1], preferred_element_type=jnp.float32) + jnp.dot(
        first_pair[1], second_pair[0], preferred_element_type=jnp.float32
    )
    return jnp.stack([real_out, imag_out])


def mirror_product(sigma_pair, tile_pair):
    contract = (((1,), (1,)), ((), ()))
    real_real = lax.dot_general(
        sigma_pair[0], tile_pair[0], contract, preferred_element_type=jnp.float32
    )
    imag_imag = lax.dot_general(
        sigma_pair[1], tile_pair[1], contract, preferred_element_type=jnp.float32
    )
    real_imag = lax.dot_general(
        sigma_pair[0], tile_pair[1], contract, preferred_element_type=jnp.float32
    )
    imag_real = lax.dot_general(
        sigma_pair[1], tile_pair[0], contract, preferred_element_type=jnp.float32
    )
    return jnp.stack([-real_real - imag_imag, real_imag - imag_real])


def self_energy(green, row_weight, col_weight):
    magnitude = green[0] * green[0] + green[1] * green[1]
    factor = -(row_weight[:, None] * col_weight[None, :]) * magnitude
    return green * factor[None]


def orbital_weights(coupling, offset, count):
    orbitals = coupling.shape[0]
    position = (offset + jnp.arange(count, dtype=jnp.int32)) % orbitals
    one_hot = (position[:, None] == jnp.arange(orbitals, dtype=jnp.int32)[None, :]).astype(
        jnp.float32
    )
    return jnp.dot(
        one_hot, coupling, precision=lax.Precision.HIGHEST, preferred_element_type=jnp.float32
    )


MESH = pl.DeviceIdType.MESH
NN = (((1,), (0,)), ((), ()))
NT = (((1,), (1,)), ((), ()))
CHUNKS = 4
(
    RELAY,
    PRODUCT,
    SOLVE,
    UPDATE,
    SPREAD_TAU,
    GIVE,
    KEEP,
    CHAIN,
    SEND_NEAR,
    RELAY_NEAR,
    NOTHING,
) = range(11)


def mm(x, y, dims):
    return lax.dot_general(x, y, dims, preferred_element_type=jnp.float32)


def remote(src, dst, send_sem, recv_sem, row, col):
    return pltpu.make_async_remote_copy(
        src_ref=src,
        dst_ref=dst,
        send_sem=send_sem,
        recv_sem=recv_sem,
        device_id=(row, col),
        device_id_type=MESH,
    )


def head_start(q, lines):
    return CHUNKS if q == 0 else min(q, CHUNKS)


COST = {
    RELAY: 0.15,
    PRODUCT: 2.2,
    SOLVE: 1.3,
    UPDATE: 2.3,
    SPREAD_TAU: 0.15,
    GIVE: 2.4,
    KEEP: 3.0,
    CHAIN: 0.5,
    SEND_NEAR: 0.1,
    RELAY_NEAR: 0.1,
}
RANK = {
    RELAY: 0,
    SPREAD_TAU: 1,
    CHAIN: 2,
    SOLVE: 3,
    PRODUCT: 4,
    KEEP: 4.5,
    GIVE: 5,
    UPDATE: 6,
    SEND_NEAR: 7,
    RELAY_NEAR: 7,
}
HOP, PLANE_SUM, PLANE_TAU, LATENCY = 22.5, 5.6, 2.8, 1.5


def plan(lines):
    last = lines - 1
    arrive, links, plane = {}, {}, [0.0] * lines
    todo, done, clock, order = [], [{} for _ in range(lines)], [0.0] * lines, []

    def hop(q, to, time, event):
        begin = max(time, links.get((q, to), 0.0))
        links[(q, to)] = begin + HOP / CHUNKS
        arrive[(to,) + event] = begin + HOP / CHUNKS + LATENCY

    def share(q, time, length, event):
        begin = max(time, plane[q])
        plane[q] = begin + length
        arrive[(q,) + event] = begin + length + LATENCY

    for q in range(lines):
        tasks = set()
        for m in range(lines):
            tasks |= {(PRODUCT, m, 0), (PRODUCT, m, 1)}
            for j in (2 * m, 2 * m + 1):
                tasks |= {(SOLVE, j, 0), (SPREAD_TAU, j, 0)}
            tasks |= {(kind, m, 0) for kind in (GIVE, KEEP, SEND_NEAR, RELAY_NEAR)}
            tasks |= {(UPDATE, m, later) for later in range(m + 1, lines)}
            if m != q:
                tasks |= {(RELAY, m, k) for k in range(CHUNKS)}
                if not ((m < q and q == last) or (m > q and q == 0)):
                    tasks |= {(CHAIN, m, k) for k in range(CHUNKS)}
        if q > 0:
            tasks |= {(CHAIN, q, k) for k in range(CHUNKS)}
        if q < last:
            tasks |= {(CHAIN, q, CHUNKS + k) for k in range(CHUNKS)}
        todo.append(tasks)
        order.append([])
        arrive[(q, "pair", q)] = 3.0
        if q > 0:
            for k in range(CHUNKS):
                hop(q, q - 1, 0.0, ("block", q, k))
        if q < last:
            for k in range(head_start(q, lines)):
                hop(q, q + 1, 0.0, ("block", q, k))

    def ready(q, task):
        kind, a, b = task
        mine = done[q]

        def got(*event):
            return arrive.get((q,) + event)

        if kind == RELAY:
            need = [got("block", a, b)]
        elif kind == PRODUCT and b == 1:
            need = [got("pair", a)]
        elif kind == PRODUCT:
            need = [0.0] if a == q else [mine.get((RELAY, a, k)) for k in range(CHUNKS)]
        elif kind == SOLVE:
            m = a // 2
            need = [got("sum", m, 0), got("sum", m, 1)]
            need += [mine.get((UPDATE, x, m)) for x in range(m)]
            need += [mine.get((SOLVE, a - 1, 0))] if a else []
        elif kind == UPDATE:
            need = [mine.get((SOLVE, 2 * a + 1, 0))]
        elif kind == SPREAD_TAU:
            need = [got("tau", a)]
        elif kind == GIVE:
            need = [got("all", 2 * a), got("all", 2 * a + 1)]
        elif kind == KEEP:
            need = [mine.get((GIVE, a, 0))]
        elif kind == CHAIN:
            need = [mine.get((KEEP, a, 0)), got("part", a, b)]
        elif kind == SEND_NEAR:
            need = [mine.get((SOLVE, 2 * a + 1, 0)), plane[q]]
        else:
            need = [got("near", a)]
        return None if None in need else max(need)

    def rank(q, task):
        kind, a, b = task
        extra = 0.1 * a - 0.5 * (a == q) if kind == PRODUCT else 0.1 * b * (kind == UPDATE)
        return RANK[kind] + extra

    while any(todo):
        best = None
        for q in range(lines):
            able = []
            for task in todo[q]:
                time = ready(q, task)
                if time is not None:
                    able.append((max(time, clock[q]), rank(q, task), task))
            if able:
                first = min(able)
                if best is None or first[0] < best[0]:
                    best = (first[0], q, first[2])
        begin, q, task = best
        kind, a, b = task
        todo[q].remove(task)
        end = begin + COST[kind]
        if kind == KEEP:
            end = max(end, arrive[(q, "give", a)] + 0.6)
        done[q][task] = end
        clock[q] = end
        order[q].append(task)
        side = q + 1 if a > q else q - 1
        if kind == RELAY:
            to = q + 1 if a < q else q - 1
            if 0 <= to <= last:
                hop(q, to, begin, ("block", a, b))
            if b == CHUNKS - 1:
                arrive[(q, "pair", a)] = end + 2.0
                if a == q - 1 and q < last:
                    for k in range(head_start(q, lines), CHUNKS):
                        hop(q, q + 1, end, ("block", q, k))
        elif kind == PRODUCT:
            share(q, end, PLANE_SUM, ("sum", a, b))
        elif kind == SOLVE:
            share(q, end, PLANE_TAU, ("tau", a))
        elif kind == SPREAD_TAU:
            share(q, end, PLANE_TAU / 2, ("all", a))
        elif kind == SEND_NEAR:
            share(q, end, 2 * PLANE_TAU, ("near", a))
        elif kind == RELAY_NEAR:
            share(q, end, PLANE_TAU, ("wide", a))
        elif kind == GIVE:
            arrive[(q, "give", a)] = end + 3.0
        elif a != q and (kind == CHAIN or (kind == KEEP and q == (last if a < q else 0))):
            for k in [b] if kind == CHAIN else range(CHUNKS):
                slot = CHUNKS + k if side == a and a < q else k
                hop(q, side, end, ("part", a, slot))
    return order


def step_words(lines):
    order = plan(lines)
    longest = max(len(steps) for steps in order)
    longest += -longest % 3
    packed = []
    for steps in order:
        codes = [kind * 64 + a * 8 + b for kind, a, b in steps]
        codes += [NOTHING * 64] * (longest - len(codes))
        packed.append(
            [
                codes[i] + 1024 * codes[i + 1] + 1024 * 1024 * codes[i + 2]
                for i in range(0, longest, 3)
            ]
        )
    return longest, packed


def entry_barrier(row, q, core, lines, rows, wait):
    barrier = pltpu.get_barrier_semaphore()
    ends = jnp.minimum(q, 1) + jnp.minimum(lines - 1 - q, 1)
    if wait:
        pl.semaphore_wait(barrier, rows + ends)
        return

    def greet(to_row, to_col):
        pl.semaphore_signal(barrier, inc=1, device_id=(to_row, to_col), device_id_type=MESH)

    greet(row, 2 * q + 1 - core)
    for k in range(1, rows):
        greet(lax.rem(row + k, rows), 2 * q + core)

    @pl.when(q > 0)
    def _():
        greet(row, 2 * (q - 1) + core)

    @pl.when(q < lines - 1)
    def _():
        greet(row, 2 * (q + 1) + core)


def fused_kernel(
    lines, rows, count, packed, strip, hist, weight, dyson, later, wide,
    blocks, parts, recv, own, new, tau, source, near, taus, give, take, stage, land, held,
    hop_s, hop_r, pair_s, pair_r, sum_s, sum_r, tau_s, tau_r, near_s, near_r, local,
    give_s, give_r, chain_s, chain_r,
):
    row = lax.axis_index("row")
    col = lax.axis_index("col")
    q, core = lax.div(col, 2), lax.rem(col, 2)
    last = lines - 1
    height, depth = strip.shape[1:]
    share = near.shape[2]
    orbitals = weight.shape[0]
    times = height // orbitals
    total = times * 2 * lines
    piece = height // CHUNKS
    beside = row + 1 - 2 * lax.rem(row, 2)
    across = lax.rem(row + 2, 4)
    direct = [beside, across]
    bf16 = jnp.bfloat16

    def span(j):
        return pl.ds(pl.multiple_of(j * height, height), height)

    def double(m):
        return pl.ds(pl.multiple_of(2 * m * height, 2 * height), 2 * height)

    def cut(k):
        return pl.ds(pl.multiple_of(k * piece, piece), piece)

    def columns(r):
        return pl.ds(pl.multiple_of(r * share, share), share)

    def slab(n):
        return pl.ds(pl.multiple_of(n * orbitals, orbitals), orbitals)

    def hop(way, m, k):
        block = blocks.at[2 * m + core, :, cut(k)]
        to = 2 * (q + 1 - 2 * way) + core
        return remote(block, block, hop_s.at[way, m, k], hop_r.at[m, k], row, to)

    def pair(m, k):
        block = blocks.at[2 * m + core, :, cut(k)]
        return remote(block, block, pair_s.at[m, k], pair_r.at[m, k], row, 2 * q + 1 - core)

    def spread(j, k):
        to = lax.rem(row + k, rows)
        return remote(
            parts.at[j, to], recv.at[j, k - 1], sum_s.at[j, k - 1], sum_r.at[j, k - 1], to, col
        )

    def send_tau(j, k):
        block = taus.at[row, :, span(j)]
        return remote(block, block, tau_s.at[j, k], tau_r.at[j, k], direct[k], col)

    def relay_tau(j, k):
        block = taus.at[direct[k], k, span(j)]
        return remote(block, block, tau_s.at[j, 2 + k], tau_r.at[j, 2 + k], direct[1 - k], col)

    def send_near(m, k):
        return remote(
            near.at[:, double(m)],
            wide.at[:, double(m), columns(row)],
            near_s.at[m, k],
            near_r.at[m, k],
            direct[k],
            col,
        )

    def relay_near(m, k):
        block = wide.at[k, double(m), columns(direct[k])]
        return remote(block, block, near_s.at[m, 2 + k], near_r.at[m, 2 + k], direct[1 - k], col)

    def own_near(m):
        return pltpu.make_async_copy(
            near.at[:, double(m)], wide.at[:, double(m), columns(row)], local.at[m]
        )

    def swap(d):
        return remote(give.at[d], take.at[d], give_s.at[d], give_r.at[d], row, 2 * q + 1 - core)

    def chain(way, d, k):
        to = q + 1 - 2 * way
        slot = jnp.where(jnp.logical_and(d == to, way == 1), lines, d)
        return remote(
            stage.at[d, :, cut(k)],
            land.at[slot, :, cut(k)],
            chain_s.at[d, k],
            chain_r.at[slot, k],
            row,
            2 * to + core,
        )

    def chain_on(d, k):
        @pl.when(d > q)
        def _():
            chain(0, d, k).start()

        @pl.when(d < q)
        def _():
            chain(1, d, k).start()

    def update(acc, src, group, low, n, j):
        def add(i, c):
            at = low + i
            real, imag = acc[0, slab(at), :], acc[1, slab(at), :]
            for t in range(times):
                m = j * times + t
                there = (2 * group * total + at) * total + m
                dr, di = dyson[there], dyson[there + total * total]
                sr, si = src[0, slab(m), :], src[1, slab(m), :]
                real += dr * sr - di * si
                imag += dr * si + di * sr
            acc[0, slab(at), :] = real
            acc[1, slab(at), :] = imag
            return c

        lax.fori_loop(0, n, add, 0)

    def op_relay(m, k):
        hop(0, m, k).wait_recv()

        @pl.when(jnp.logical_and(m < q, q < last))
        def _():
            hop(0, m, k).start()

        @pl.when(jnp.logical_and(m > q, q > 0))
        def _():
            hop(1, m, k).start()

        pair(m, k).start()

        @pl.when(jnp.logical_and(m == q - 1, k == CHUNKS - 1))
        def _():
            rest()

    def rest():
        for x in range(CHUNKS):

            @pl.when(jnp.logical_and(q < last, jnp.logical_and(q > 0, x >= q)))
            def _():
                hop(0, q, x).start()

    def op_product(m, other):
        @pl.when(other == 1)
        def _():
            for k in range(CHUNKS):
                pair(m, k).wait_recv()

        j = 2 * m + core + other - 2 * core * other
        real = mm(blocks[j, 0], hist[0], NN) - mm(blocks[j, 1], hist[1], NN)
        imag = mm(blocks[j, 0], hist[1], NN) + mm(blocks[j, 1], hist[0], NN)
        for r in range(rows):
            part = slice(r * share, (r + 1) * share)
            parts[j, r, 0] = real[:, part].astype(bf16)
            parts[j, r, 1] = imag[:, part].astype(bf16)

            @pl.when(row == r)
            def _():
                own[0, span(j), :] = real[:, part]
                own[1, span(j), :] = imag[:, part]

        for k in range(1, rows):
            spread(j, k).start()

    def op_solve(j):
        at = span(j)
        for k in range(1, rows):
            spread(j, k).wait_recv()
        for p in (0, 1):
            value = own[p, at, :]
            for k in range(1, rows):
                value += recv[j, k - 1, p].astype(jnp.float32)
            own[p, at, :] = TIME_STEP * value

        @pl.when(lax.rem(j, 2) == 1)
        def _():
            update(new, own, 0, j * times, times, j - 1)

        update(new, own, 0, j * times, times, j)

        def sigma(i, c):
            rows_at = slab(j * times + i)
            real, imag = new[0, rows_at, :], new[1, rows_at, :]
            near[0, rows_at, :] = real.astype(bf16)
            near[1, rows_at, :] = imag.astype(bf16)
            factor = weight[...] * (real * real + imag * imag)
            source[0, rows_at, :] = TIME_STEP * (real * factor).astype(bf16).astype(jnp.float32)
            source[1, rows_at, :] = TIME_STEP * (imag * factor).astype(bf16).astype(jnp.float32)
            return c

        lax.fori_loop(0, times, sigma, 0)

        @pl.when(lax.rem(j, 2) == 1)
        def _():
            update(tau, source, 1, j * times, times, j - 1)

        update(tau, source, 1, j * times, times, j)
        for p in (0, 1):
            taus[row, p, at, :] = tau[p, at, :].astype(bf16)
        for k in (0, 1):
            send_tau(j, k).start()

    def op_update(m, later_m):
        def both(half, c):
            update(new, own, 0, 2 * times * later_m, 2 * times, 2 * m + half)
            update(tau, source, 1, 2 * times * later_m, 2 * times, 2 * m + half)
            return c

        lax.fori_loop(0, 2, both, 0)

    def op_spread_tau(j):
        for k in (0, 1):
            send_tau(j, k).wait_recv()
        for k in (0, 1):
            relay_tau(j, k).start()

    def second(j):
        for k in (0, 1):
            relay_tau(j, k).wait_recv()
        at = span(j)
        real_in = jnp.concatenate([taus[r, 0, at, :] for r in range(rows)], axis=1)
        imag_in = jnp.concatenate([taus[r, 1, at, :] for r in range(rows)], axis=1)
        real = -mm(real_in, hist[0], NT) - mm(imag_in, hist[1], NT)
        imag = mm(real_in, hist[1], NT) - mm(imag_in, hist[0], NT)
        return real, imag

    def held_at(d):
        return d - jnp.where(d > q, 1, 0)

    def op_second(d, keep):
        pair_sums = second(2 * d + core + (1 - keep) * (1 - 2 * core))

        @pl.when(keep == 0)
        def _():
            for p in (0, 1):
                give[d, p] = pair_sums[p].astype(bf16)
            swap(d).start()

        @pl.when(keep == 1)
        def _():
            swap(d).wait_recv()
            begins = jnp.logical_or(
                jnp.logical_and(d < q, q == last), jnp.logical_and(d > q, q == 0)
            )

            @pl.when(d == q)
            def _():
                for p in (0, 1):
                    later[p] = pair_sums[p] + take[d, p].astype(jnp.float32)

            @pl.when(begins)
            def _():
                for p in (0, 1):
                    value = pair_sums[p] + take[d, p].astype(jnp.float32)
                    stage[d, p] = value.astype(bf16)
                for k in range(CHUNKS):
                    chain_on(d, k)

            @pl.when(jnp.logical_and(d != q, jnp.logical_not(begins)))
            def _():
                for p in (0, 1):
                    held[held_at(d), p] = pair_sums[p] + take[d, p].astype(jnp.float32)

    def op_chain(d, b):
        way, k = lax.div(b, CHUNKS), lax.rem(b, CHUNKS)
        at = cut(k)
        slot = jnp.where(way == 1, lines, d)
        pltpu.make_async_remote_copy(
            src_ref=stage.at[d, :, at],
            dst_ref=land.at[slot, :, at],
            send_sem=chain_s.at[d, k],
            recv_sem=chain_r.at[slot, k],
            device_id=(row, 2 * q + 1 - core),
            device_id_type=MESH,
        ).wait_recv()

        @pl.when(d == q)
        def _():
            for p in (0, 1):
                later[p, at, :] += land[slot, p, at, :].astype(jnp.float32)

        @pl.when(d != q)
        def _():
            for p in (0, 1):
                value = held[held_at(d), p, at, :] + land[slot, p, at, :].astype(jnp.float32)
                stage[d, p, at, :] = value.astype(bf16)
            chain_on(d, k)

    def op_send_near(m):
        own_near(m).start()
        for k in (0, 1):
            send_near(m, k).start()

    def op_relay_near(m):
        for k in (0, 1):
            send_near(m, k).wait_recv()
        for k in (0, 1):
            relay_near(m, k).start()

    entry_barrier(row, q, core, lines, rows, False)

    def fill(i, c):
        at = slab(i)
        scale = jnp.concatenate([weight[...]] * (depth // weight.shape[1]), axis=1)
        real, imag = strip[0, at, :], strip[1, at, :]
        factor = scale * (real * real + imag * imag)
        blocks[col, 0, at, :] = (real * factor).astype(bf16)
        blocks[col, 1, at, :] = (imag * factor).astype(bf16)
        return c

    lax.fori_loop(0, times, fill, 0)
    entry_barrier(row, q, core, lines, rows, True)

    for x in range(CHUNKS):

        @pl.when(jnp.logical_and(q < last, jnp.logical_or(q == 0, x < q)))
        def _():
            hop(0, q, x).start()

    for x in range(CHUNKS):

        @pl.when(q > 0)
        def _():
            hop(1, q, x).start()

    for x in range(CHUNKS):
        pair(q, x).start()

    def clear(n, c):
        for p in (0, 1):
            new[p, slab(n), :] = jnp.zeros((orbitals, share), jnp.float32)
            tau[p, slab(n), :] = jnp.zeros((orbitals, share), jnp.float32)
        return c

    lax.fori_loop(0, total, clear, 0)

    words = []
    for w in range(count // 3):
        word = jnp.int32(packed[last][w])
        for x in range(last):
            word = jnp.where(q == x, jnp.int32(packed[x][w]), word)
        words.append(word)

    def step(i, c):
        which, place = lax.div(i, 3), lax.rem(i, 3)
        word = words[0]
        for w in range(1, len(words)):
            word = jnp.where(which == w, words[w], word)
        middle = lax.rem(lax.div(word, 1024), 1024)
        code = jnp.where(place == 1, middle, lax.rem(word, 1024))
        code = jnp.where(place == 2, lax.div(word, 1024 * 1024), code)
        kind, a, b = lax.div(code, 64), lax.rem(lax.div(code, 8), 8), lax.rem(code, 8)

        @pl.when(kind == RELAY)
        def _():
            op_relay(a, b)

        @pl.when(kind == PRODUCT)
        def _():
            op_product(a, b)

        @pl.when(kind == SOLVE)
        def _():
            op_solve(a)

        @pl.when(kind == UPDATE)
        def _():
            op_update(a, b)

        @pl.when(kind == SPREAD_TAU)
        def _():
            op_spread_tau(a)

        @pl.when(jnp.logical_or(kind == GIVE, kind == KEEP))
        def _():
            op_second(a, kind - GIVE)

        @pl.when(kind == CHAIN)
        def _():
            op_chain(a, b)

        @pl.when(kind == SEND_NEAR)
        def _():
            op_send_near(a)

        @pl.when(kind == RELAY_NEAR)
        def _():
            op_relay_near(a)

        return c

    lax.fori_loop(0, count, step, 0)

    def drain_line(m, c):
        for k in range(CHUNKS):

            @pl.when(jnp.logical_and(m <= q, q < last))
            def _():
                hop(0, m, k).wait_send()

            @pl.when(jnp.logical_and(m >= q, q > 0))
            def _():
                hop(1, m, k).wait_send()

            pair(m, k).wait_send()

            @pl.when(m != q)
            def _():
                chain(0, m, k).wait_send()

        swap(m).wait_send()
        own_near(m).wait()
        for k in (0, 1):
            send_near(m, k).wait_send()
            relay_near(m, k).wait()
        return c

    lax.fori_loop(0, lines, drain_line, 0)

    def drain_block(j, c):
        for k in range(1, rows):
            spread(j, k).wait_send()
        for k in (0, 1):
            send_tau(j, k).wait_send()
            relay_tau(j, k).wait_send()
        return c

    lax.fori_loop(0, 2 * lines, drain_block, 0)


VMEM = pl.BlockSpec(memory_space=pltpu.VMEM)
DMA = pltpu.SemaphoreType.DMA


def fused(strip, history, weight, dyson, lines, rows):
    height, depth = strip.shape[1:]
    width = history.shape[2]
    share = width // rows
    blocks = 2 * lines
    full = blocks * height
    count, packed = step_words(lines)
    bf16, f32 = jnp.bfloat16, jnp.float32
    return pl.pallas_call(
        functools.partial(fused_kernel, lines, rows, count, packed),
        out_shape=(
            jax.ShapeDtypeStruct(strip.shape, f32),
            jax.ShapeDtypeStruct((2, full, width), bf16),
        ),
        in_specs=[VMEM, VMEM, VMEM, pl.BlockSpec(memory_space=pltpu.SMEM)],
        out_specs=(VMEM, pl.BlockSpec(memory_space=pl.ANY)),
        scratch_shapes=[
            pltpu.VMEM((blocks, 2, height, depth), bf16),
            pltpu.VMEM((blocks, rows, 2, height, share), bf16),
            pltpu.VMEM((blocks, rows - 1, 2, height, share), bf16),
            pltpu.VMEM((2, full, share), f32),
            pltpu.VMEM((2, full, share), f32),
            pltpu.VMEM((2, full, share), f32),
            pltpu.VMEM((2, full, share), f32),
            pltpu.VMEM((2, full, share), bf16),
            pltpu.VMEM((rows, 2, full, share), bf16),
            pltpu.VMEM((lines, 2, height, depth), bf16),
            pltpu.VMEM((lines, 2, height, depth), bf16),
            pltpu.VMEM((lines, 2, height, depth), bf16),
            pltpu.VMEM((lines + 1, 2, height, depth), bf16),
            pltpu.VMEM((lines - 1, 2, height, depth), f32),
            DMA((2, lines, CHUNKS)),
            DMA((lines, CHUNKS)),
            DMA((lines, CHUNKS)),
            DMA((lines, CHUNKS)),
            DMA((blocks, rows - 1)),
            DMA((blocks, rows - 1)),
            DMA((blocks, 4)),
            DMA((blocks, 4)),
            DMA((lines, 4)),
            DMA((lines, 4)),
            DMA((lines,)),
            DMA((lines,)),
            DMA((lines,)),
            DMA((lines, CHUNKS)),
            DMA((lines + 1, CHUNKS)),
        ],
        compiler_params=pltpu.CompilerParams(
            collective_id=0, has_side_effects=True, vmem_limit_bytes=63 * 1024 * 1024
        ),
        name="group_updates",
    )(strip, history, weight, dyson)


def stacked_dyson(inverse, source):
    group_len = inverse.shape[1]
    matrix = TIME_STEP * jnp.concatenate(
        [
            jnp.concatenate([inverse[0], -inverse[1]], axis=1),
            jnp.concatenate([inverse[1], inverse[0]], axis=1),
        ],
        axis=0,
    )
    flat = source.reshape(2 * group_len, -1)
    solved = jnp.dot(
        matrix, flat, precision=lax.Precision.HIGHEST, preferred_element_type=jnp.float32
    )
    return solved.reshape(source.shape)


def shards(history, start_strip, coupling, dyson_inverse):
    row_count = lax.axis_size("row")
    col_count = lax.axis_size("col")
    row_index = lax.axis_index("row")
    col_index = lax.axis_index("col")
    strip_rows = start_strip.shape[1]
    strip_cols = start_strip.shape[2]
    group_rows = strip_rows * col_count
    tile_cols = history.shape[2]
    share_cols = tile_cols // row_count
    orbitals = coupling.shape[0]
    fits = (
        row_count == 4
        and col_count <= 8
        and share_cols == 128
        and share_cols % orbitals == 0
        and strip_rows % (16 * CHUNKS) == 0
        and strip_rows % orbitals == 0
        and group_rows // orbitals == dyson_inverse.shape[2]
    )
    if fits:
        weight = -(coupling[:, None] * jnp.tile(coupling, share_cols // orbitals)[None, :])
        later_strip, wide = fused(
            start_strip, history, weight, dyson_inverse.reshape(-1), col_count // 2, row_count
        )
        return (wide.astype(jnp.float32), later_strip)
    sigma_first = self_energy(
        start_strip,
        orbital_weights(coupling, col_index * strip_rows, strip_rows),
        orbital_weights(coupling, row_index * strip_cols, strip_cols),
    ).astype(jnp.bfloat16)
    partial_first = complex_product(
        lax.all_gather(sigma_first, "col", axis=1, tiled=True), history
    )
    shares = lax.psum_scatter(partial_first, "row", scatter_dimension=2, tiled=True)
    solved_part = stacked_dyson(dyson_inverse[0], shares)
    sigma_second = self_energy(
        solved_part,
        orbital_weights(coupling, 0, group_rows),
        orbital_weights(coupling, col_index * tile_cols + row_index * share_cols, share_cols),
    ).astype(jnp.bfloat16)
    solved_sigma = stacked_dyson(
        dyson_inverse[1], sigma_second.astype(jnp.float32)
    ).astype(jnp.bfloat16)
    earlier = lax.all_gather(solved_part, "row", axis=2, tiled=True)
    tau = lax.all_gather(solved_sigma, "row", axis=2, tiled=True)
    partial_second = mirror_product(tau, history)
    later_strip = lax.psum_scatter(partial_second, "col", scatter_dimension=1, tiled=True)
    return (earlier, later_strip)


def solution(mesh):
    return jax.shard_map(
        shards,
        mesh=mesh,
        in_specs=(P(None, "row", "col"), P(None, "col", "row"), P(), P()),
        out_specs=(P(None, None, "col"), P(None, "col", "row")),
        check_vma=False,
    )
```

```python
import functools

import jax
import jax.numpy as jnp
from jax import lax
from jax.experimental import pallas as pl
from jax.experimental.pallas import tpu as pltpu
from jax.sharding import PartitionSpec as P

TIME_STEP = 0.15


def complex_product(first_pair, second_pair):
    real_out = jnp.dot(first_pair[0], second_pair[0], preferred_element_type=jnp.float32) - jnp.dot(
        first_pair[1], second_pair[1], preferred_element_type=jnp.float32
    )
    imag_out = jnp.dot(first_pair[0], second_pair[1], preferred_element_type=jnp.float32) + jnp.dot(
        first_pair[1], second_pair[0], preferred_element_type=jnp.float32
    )
    return jnp.stack([real_out, imag_out])


def mirror_product(sigma_pair, tile_pair):
    contract = (((1,), (1,)), ((), ()))
    real_real = lax.dot_general(
        sigma_pair[0], tile_pair[0], contract, preferred_element_type=jnp.float32
    )
    imag_imag = lax.dot_general(
        sigma_pair[1], tile_pair[1], contract, preferred_element_type=jnp.float32
    )
    real_imag = lax.dot_general(
        sigma_pair[0], tile_pair[1], contract, preferred_element_type=jnp.float32
    )
    imag_real = lax.dot_general(
        sigma_pair[1], tile_pair[0], contract, preferred_element_type=jnp.float32
    )
    return jnp.stack([-real_real - imag_imag, real_imag - imag_real])


def self_energy(green, row_weight, col_weight):
    magnitude = green[0] * green[0] + green[1] * green[1]
    factor = -(row_weight[:, None] * col_weight[None, :]) * magnitude
    return green * factor[None]


def orbital_weights(coupling, offset, count):
    orbitals = coupling.shape[0]
    position = (offset + jnp.arange(count, dtype=jnp.int32)) % orbitals
    one_hot = (position[:, None] == jnp.arange(orbitals, dtype=jnp.int32)[None, :]).astype(
        jnp.float32
    )
    return jnp.dot(
        one_hot, coupling, precision=lax.Precision.HIGHEST, preferred_element_type=jnp.float32
    )


MESH = pl.DeviceIdType.MESH
NN = (((1,), (0,)), ((), ()))
NT = (((1,), (1,)), ((), ()))
CHUNKS = 4
HEAD = 4
(
    RELAY,
    PRODUCT,
    SOLVE,
    UPDATE,
    SPREAD_TAU,
    GIVE,
    KEEP,
    CHAIN,
    SEND_NEAR,
    RELAY_NEAR,
    JOIN,
    NOTHING,
) = range(12)


def mm(x, y, dims):
    return lax.dot_general(x, y, dims, preferred_element_type=jnp.float32)


def remote(src, dst, send_sem, recv_sem, row, col):
    return pltpu.make_async_remote_copy(
        src_ref=src,
        dst_ref=dst,
        send_sem=send_sem,
        recv_sem=recv_sem,
        device_id=(row, col),
        device_id_type=MESH,
    )


ORDERS = {
    4: (
        (
            128, 129, 1280, 1281, 256, 272, 18, 1024, 17, 386, 16, 19, 144, 145,
            385, 1296, 32, 1297, 288, 304, 544, 35, 402, 560, 34, 33, 161, 656,
            160, 784, 1313, 1312, 51, 403, 320, 336, 50, 387, 576, 48, 49, 592,
            176, 177, 672, 1328, 800, 1329, 419, 528, 352, 368, 608, 624, 1072, 1056,
            688, 1152, 816, 1040, 512, 640, 1168, 768, 900, 901, 1184, 903, 1200, 902,
        ),
        (
            0, 145, 144, 32, 1, 2, 34, 35, 1296, 3, 33, 129, 128, 1280,
            160, 1281, 1297, 50, 161, 256, 51, 272, 385, 288, 48, 1313, 304, 1312,
            49, 177, 512, 402, 386, 528, 176, 320, 336, 576, 1329, 544, 419, 592,
            640, 1040, 1328, 403, 560, 672, 387, 800, 928, 768, 352, 368, 608, 930,
            624, 896, 1072, 1168, 656, 931, 688, 816, 899, 944, 945, 784, 1056, 897,
            898, 946, 1024, 914, 913, 916, 1200, 915, 947, 1152, 918, 912, 929, 1184,
            919, 917,
        ),
        (
            16, 160, 0, 50, 1, 49, 51, 161, 2, 3, 1313, 48, 128, 17,
            129, 176, 1312, 18, 1281, 1280, 177, 19, 256, 145, 144, 272, 512, 387,
            386, 528, 1296, 1329, 1297, 385, 1328, 640, 288, 304, 402, 320, 560, 336,
            403, 768, 896, 419, 576, 544, 897, 352, 368, 899, 898, 608, 592, 656,
            624, 1040, 784, 688, 1072, 912, 672, 1024, 1056, 913, 816, 1168, 914, 944,
            945, 915, 800, 946, 1152, 930, 1184, 928, 931, 1200, 947, 932, 934, 933,
            929, 935,
        ),
        (
            16, 0, 176, 32, 2, 1328, 1, 177, 3, 128, 129, 1280, 17, 1281,
            1329, 256, 18, 272, 386, 512, 19, 528, 144, 33, 34, 145, 640, 35,
            1296, 160, 768, 1297, 161, 385, 288, 304, 1312, 544, 402, 560, 1313, 1040,
            656, 320, 784, 336, 387, 1024, 592, 576, 1056, 419, 403, 352, 672, 368,
            1168, 800, 624, 608, 1072, 1184, 688, 1152, 816, 1200, 944, 946, 945, 947,
        ),
    ),
}

def step_words(lines):
    longest = max(len(steps) for steps in ORDERS[lines])
    longest += longest % 2
    packed = []
    for steps in ORDERS[lines]:
        codes = list(steps) + [NOTHING * 128] * (longest - len(steps))
        packed.append([codes[i] + 2048 * codes[i + 1] for i in range(0, longest, 2)])
    return longest, packed


def entry_barrier(row, q, core, lines, rows, wait):
    barrier = pltpu.get_barrier_semaphore()
    ends = jnp.minimum(q, 1) + jnp.minimum(lines - 1 - q, 1)
    if wait:
        pl.semaphore_wait(barrier, rows + ends)
        return

    def greet(to_row, to_col):
        pl.semaphore_signal(barrier, inc=1, device_id=(to_row, to_col), device_id_type=MESH)

    greet(row, 2 * q + 1 - core)
    for k in range(1, rows):
        greet(lax.rem(row + k, rows), 2 * q + core)

    @pl.when(q > 0)
    def _():
        greet(row, 2 * (q - 1) + core)

    @pl.when(q < lines - 1)
    def _():
        greet(row, 2 * (q + 1) + core)


def fused_kernel(
    lines, rows, count, packed, strip, history, coupling, dyson, later_out, wide,
    later, hist, weight, blocks, parts, first, keep, sums, joined, own, new, tau, source, near, taus,
    give, take, stage, land, held,
    hop_s, hop_r, pair_s, pair_r, sum_s, sum_r, tau_s, tau_r, near_s, near_r, local,
    give_s, give_r, chain_s, chain_r,
):
    row = lax.axis_index("row")
    col = lax.axis_index("col")
    q, core = lax.div(col, 2), lax.rem(col, 2)
    last = lines - 1
    height, depth = later.shape[1:]
    share = own.shape[2]
    orbitals = weight.shape[0]
    times = height // orbitals
    total = times * 2 * lines
    piece = height // CHUNKS
    beside = row + 1 - 2 * lax.rem(row, 2)
    across = lax.rem(row + 2, 4)
    direct = [beside, across]
    bf16 = jnp.bfloat16

    def head_start(at):
        return lax.div(at * CHUNKS, HEAD)

    def span(j):
        return pl.ds(pl.multiple_of(j * height, height), height)

    def double(m):
        return pl.ds(pl.multiple_of(2 * m * height, 2 * height), 2 * height)

    def cut(k):
        return pl.ds(pl.multiple_of(k * piece, piece), piece)

    def columns(r):
        return pl.ds(pl.multiple_of(r * share, share), share)

    def slab(n):
        return pl.ds(pl.multiple_of(n * orbitals, orbitals), orbitals)

    def hop(way, m, k):
        block = blocks.at[2 * m + core, :, cut(k)]
        to = 2 * (q + 1 - 2 * way) + core
        return remote(block, block, hop_s.at[way, m, k], hop_r.at[m, k], row, to)

    def pair(m, k):
        block = blocks.at[2 * m + core, :, cut(k)]
        return remote(block, block, pair_s.at[m, k], pair_r.at[m, k], row, 2 * q + 1 - core)

    def send_parts(j, k):
        return remote(
            parts.at[j, k], first.at[j, k], sum_s.at[j, k], sum_r.at[j, k], direct[k], col
        )

    def send_joined(j, k):
        return remote(
            sums.at[j, k], joined.at[j, k], sum_s.at[j, 2 + k], sum_r.at[j, 2 + k],
            direct[1 - k], col,
        )

    def send_tau(j, k):
        block = taus.at[row, :, span(j)]
        return remote(block, block, tau_s.at[j, k], tau_r.at[j, k], direct[k], col)

    def relay_tau(j, k):
        block = taus.at[direct[k], k, span(j)]
        return remote(block, block, tau_s.at[j, 2 + k], tau_r.at[j, 2 + k], direct[1 - k], col)

    def send_near(m, k):
        return remote(
            near.at[:, double(m)],
            wide.at[:, double(m), columns(row)],
            near_s.at[m, k],
            near_r.at[m, k],
            direct[k],
            col,
        )

    def relay_near(m, k):
        block = wide.at[k, double(m), columns(direct[k])]
        return remote(block, block, near_s.at[m, 2 + k], near_r.at[m, 2 + k], direct[1 - k], col)

    def own_near(m):
        return pltpu.make_async_copy(
            near.at[:, double(m)], wide.at[:, double(m), columns(row)], local.at[m]
        )

    def swap(d):
        return remote(give.at[d], take.at[d], give_s.at[d], give_r.at[d], row, 2 * q + 1 - core)

    def chain(way, d, k):
        to = q + 1 - 2 * way
        slot = jnp.where(jnp.logical_and(d == to, way == 1), lines, d)
        return remote(
            stage.at[d, :, cut(k)],
            land.at[slot, :, cut(k)],
            chain_s.at[d, k],
            chain_r.at[slot, k],
            row,
            2 * to + core,
        )

    def chain_on(d, k):
        @pl.when(d > q)
        def _():
            chain(0, d, k).start()

        @pl.when(d < q)
        def _():
            chain(1, d, k).start()

    def update(acc, src, group, low, n, j):
        def add(i, c):
            at = low + i
            real, imag = acc[0, slab(at), :], acc[1, slab(at), :]
            for t in range(times):
                m = j * times + t
                dr, di = dyson[group, 0, at, m], dyson[group, 1, at, m]
                sr = src[0, slab(m), :].astype(jnp.float32)
                si = src[1, slab(m), :].astype(jnp.float32)
                real += dr * sr - di * si
                imag += dr * si + di * sr
            acc[0, slab(at), :] = real
            acc[1, slab(at), :] = imag
            return c

        lax.fori_loop(0, n, add, 0)

    def op_relay(m, k):
        hop(0, m, k).wait_recv()

        @pl.when(jnp.logical_and(m < q, q < last))
        def _():
            hop(0, m, k).start()

        @pl.when(jnp.logical_and(m > q, q > 0))
        def _():
            hop(1, m, k).start()

        pair(m, k).start()

        @pl.when(jnp.logical_and(m == q - 1, k == CHUNKS - 1))
        def _():
            rest()

    def rest():
        for x in range(CHUNKS):

            @pl.when(jnp.logical_and(q < last, jnp.logical_and(q > 0, x >= head_start(q))))
            def _():
                hop(0, q, x).start()

    def op_product(m, other):
        @pl.when(other == 1)
        def _():
            for k in range(CHUNKS):
                pair(m, k).wait_recv()

        j = 2 * m + core + other - 2 * core * other
        real = mm(blocks[j, 0], hist[0], NN) - mm(blocks[j, 1], hist[1], NN)
        imag = mm(blocks[j, 0], hist[1], NN) + mm(blocks[j, 1], hist[0], NN)
        for r in range(rows):

            @pl.when(row == r)
            def _():
                mine, near_x, near_y, far = [
                    slice(x * share, (x + 1) * share) for x in (r, r ^ 1, r ^ 2, r ^ 3)
                ]
                parts[j, 0, 0] = real[:, near_x].astype(bf16)
                parts[j, 0, 1] = real[:, far].astype(bf16)
                parts[j, 1, 0] = imag[:, near_y].astype(bf16)
                parts[j, 1, 1] = imag[:, far].astype(bf16)
                keep[j, 0] = real[:, near_y]
                keep[j, 1] = imag[:, near_x]
                own[0, span(j), :] = real[:, mine]
                own[1, span(j), :] = imag[:, mine]

        for k in (0, 1):
            send_parts(j, k).start()

    def op_join(m, other):
        j = 2 * m + core + other - 2 * core * other
        for k in (0, 1):
            send_parts(j, k).wait_recv()
            sums[j, k] = (keep[j, k] + first[j, k, 1].astype(jnp.float32)).astype(bf16)
        for k in (0, 1):
            send_joined(j, k).start()

    def op_solve(j):
        at = span(j)
        for p in (0, 1):
            send_joined(j, p).wait_recv()
            others = first[j, p, 0].astype(jnp.float32) + joined[j, p].astype(jnp.float32)
            own[p, at, :] = TIME_STEP * (own[p, at, :] + others)

        @pl.when(lax.rem(j, 2) == 1)
        def _():
            update(new, own, 0, j * times, times, j - 1)

        update(new, own, 0, j * times, times, j)

        def sigma(i, c):
            rows_at = slab(j * times + i)
            real, imag = new[0, rows_at, :], new[1, rows_at, :]
            near[0, rows_at, :] = real.astype(bf16)
            near[1, rows_at, :] = imag.astype(bf16)
            factor = weight[...] * (real * real + imag * imag)
            source[0, rows_at, :] = (real * factor).astype(bf16)
            source[1, rows_at, :] = (imag * factor).astype(bf16)
            return c

        lax.fori_loop(0, times, sigma, 0)

        @pl.when(lax.rem(j, 2) == 1)
        def _():
            update(tau, source, 1, j * times, times, j - 1)

        update(tau, source, 1, j * times, times, j)
        for p in (0, 1):
            taus[row, p, at, :] = (TIME_STEP * tau[p, at, :]).astype(bf16)
        for k in (0, 1):
            send_tau(j, k).start()

    def op_update(m, later_m):
        def both(half, c):
            update(new, own, 0, 2 * times * later_m, 2 * times, 2 * m + half)
            update(tau, source, 1, 2 * times * later_m, 2 * times, 2 * m + half)
            return c

        lax.fori_loop(0, 2, both, 0)

    def op_spread_tau(j):
        for k in (0, 1):
            send_tau(j, k).wait_recv()
        for k in (0, 1):
            relay_tau(j, k).start()

    def second(j):
        for k in (0, 1):
            relay_tau(j, k).wait_recv()
        at = span(j)
        real_in = jnp.concatenate([taus[r, 0, at, :] for r in range(rows)], axis=1)
        imag_in = jnp.concatenate([taus[r, 1, at, :] for r in range(rows)], axis=1)
        real = -mm(real_in, hist[0], NT) - mm(imag_in, hist[1], NT)
        imag = mm(real_in, hist[1], NT) - mm(imag_in, hist[0], NT)
        return real, imag

    def held_at(d):
        return d - jnp.where(d > q, 1, 0)

    def op_second(d, keep):
        pair_sums = second(2 * d + core + (1 - keep) * (1 - 2 * core))

        @pl.when(keep == 0)
        def _():
            for p in (0, 1):
                give[d, p] = pair_sums[p].astype(bf16)
            swap(d).start()

        @pl.when(keep == 1)
        def _():
            swap(d).wait_recv()
            begins = jnp.logical_or(
                jnp.logical_and(d < q, q == last), jnp.logical_and(d > q, q == 0)
            )

            @pl.when(d == q)
            def _():
                for p in (0, 1):
                    later[p] = pair_sums[p] + take[d, p].astype(jnp.float32)

            @pl.when(begins)
            def _():
                for p in (0, 1):
                    value = pair_sums[p] + take[d, p].astype(jnp.float32)
                    stage[d, p] = value.astype(bf16)
                for k in range(CHUNKS):
                    chain_on(d, k)

            @pl.when(jnp.logical_and(d != q, jnp.logical_not(begins)))
            def _():
                for p in (0, 1):
                    held[held_at(d), p] = pair_sums[p] + take[d, p].astype(jnp.float32)

    def op_chain(d, b):
        way, k = lax.div(b, CHUNKS), lax.rem(b, CHUNKS)
        at = cut(k)
        slot = jnp.where(way == 1, lines, d)
        pltpu.make_async_remote_copy(
            src_ref=stage.at[d, :, at],
            dst_ref=land.at[slot, :, at],
            send_sem=chain_s.at[d, k],
            recv_sem=chain_r.at[slot, k],
            device_id=(row, 2 * q + 1 - core),
            device_id_type=MESH,
        ).wait_recv()

        @pl.when(d == q)
        def _():
            for p in (0, 1):
                later[p, at, :] += land[slot, p, at, :].astype(jnp.float32)

        @pl.when(d != q)
        def _():
            for p in (0, 1):
                value = held[held_at(d), p, at, :] + land[slot, p, at, :].astype(jnp.float32)
                stage[d, p, at, :] = value.astype(bf16)
            chain_on(d, k)

    def op_send_near(m):
        own_near(m).start()
        for k in (0, 1):
            send_near(m, k).start()

    def op_relay_near(m):
        for k in (0, 1):
            send_near(m, k).wait_recv()
        for k in (0, 1):
            relay_near(m, k).start()

    load_hist = pltpu.make_async_copy(history, hist, local.at[lines])
    load_strip = pltpu.make_async_copy(strip, later, local.at[lines + 1])
    load_strip.start()
    load_hist.start()
    entry_barrier(row, q, core, lines, rows, False)
    place_row = lax.broadcasted_iota(jnp.int32, (orbitals, share), 0)
    place_col = lax.rem(lax.broadcasted_iota(jnp.int32, (orbitals, share), 1), orbitals)
    down = jnp.zeros((orbitals, share), jnp.float32)
    along = jnp.zeros((orbitals, share), jnp.float32)
    for a in range(orbitals):
        down = jnp.where(place_row == a, coupling[a], down)
        along = jnp.where(place_col == a, coupling[a], along)
    weight[...] = -(down * along)
    load_strip.wait()

    def fill(i, c):
        at = slab(i)
        scale = jnp.concatenate([weight[...]] * (depth // share), axis=1)
        real, imag = later[0, at, :], later[1, at, :]
        factor = scale * (real * real + imag * imag)
        blocks[col, 0, at, :] = (real * factor).astype(bf16)
        blocks[col, 1, at, :] = (imag * factor).astype(bf16)
        return c

    lax.fori_loop(0, times, fill, 0)
    entry_barrier(row, q, core, lines, rows, True)

    for x in range(CHUNKS):

        @pl.when(jnp.logical_and(q < last, jnp.logical_or(q == 0, x < head_start(q))))
        def _():
            hop(0, q, x).start()

    for x in range(CHUNKS):

        @pl.when(q > 0)
        def _():
            hop(1, q, x).start()

    for x in range(CHUNKS):
        pair(q, x).start()

    def clear(n, c):
        for p in (0, 1):
            new[p, slab(n), :] = jnp.zeros((orbitals, share), jnp.float32)
            tau[p, slab(n), :] = jnp.zeros((orbitals, share), jnp.float32)
        return c

    lax.fori_loop(0, total, clear, 0)
    load_hist.wait()

    words = []
    for w in range(count // 2):
        word = jnp.int32(packed[last][w])
        for x in range(last):
            word = jnp.where(q == x, jnp.int32(packed[x][w]), word)
        words.append(word)

    def step(i, c):
        which, place = lax.div(i, 2), lax.rem(i, 2)
        word = words[0]
        for w in range(1, len(words)):
            word = jnp.where(which == w, words[w], word)
        code = jnp.where(place == 1, lax.div(word, 2048), lax.rem(word, 2048))
        kind, a, b = lax.div(code, 128), lax.rem(lax.div(code, 16), 8), lax.rem(code, 16)

        @pl.when(kind == RELAY)
        def _():
            op_relay(a, b)

        @pl.when(kind == PRODUCT)
        def _():
            op_product(a, b)

        @pl.when(kind == JOIN)
        def _():
            op_join(a, b)

        @pl.when(kind == SOLVE)
        def _():
            op_solve(a)

        @pl.when(kind == UPDATE)
        def _():
            op_update(a, b)

        @pl.when(kind == SPREAD_TAU)
        def _():
            op_spread_tau(a)

        @pl.when(jnp.logical_or(kind == GIVE, kind == KEEP))
        def _():
            op_second(a, kind - GIVE)

        @pl.when(kind == CHAIN)
        def _():
            op_chain(a, b)

        @pl.when(kind == SEND_NEAR)
        def _():
            op_send_near(a)

        @pl.when(kind == RELAY_NEAR)
        def _():
            op_relay_near(a)

        return c

    lax.fori_loop(0, count, step, 0)
    leave = pltpu.make_async_copy(later, later_out, local.at[lines])
    leave.start()

    def drain_line(m, c):
        for k in range(CHUNKS):

            @pl.when(jnp.logical_and(m <= q, q < last))
            def _():
                hop(0, m, k).wait_send()

            @pl.when(jnp.logical_and(m >= q, q > 0))
            def _():
                hop(1, m, k).wait_send()

            pair(m, k).wait_send()

            @pl.when(m != q)
            def _():
                chain(0, m, k).wait_send()

        swap(m).wait_send()
        own_near(m).wait()
        for k in (0, 1):
            send_near(m, k).wait_send()
            relay_near(m, k).wait()
        return c

    lax.fori_loop(0, lines, drain_line, 0)

    def drain_block(j, c):
        for k in (0, 1):
            send_parts(j, k).wait_send()
            send_joined(j, k).wait_send()
            send_tau(j, k).wait_send()
            relay_tau(j, k).wait_send()
        return c

    lax.fori_loop(0, 2 * lines, drain_block, 0)
    leave.wait()


VMEM = pl.BlockSpec(memory_space=pltpu.VMEM)
ANY = pl.BlockSpec(memory_space=pl.ANY)
SMEM = pl.BlockSpec(memory_space=pltpu.SMEM)
DMA = pltpu.SemaphoreType.DMA


def fused(strip, history, coupling, dyson, lines, rows):
    height, depth = strip.shape[1:]
    width = history.shape[2]
    share = width // rows
    blocks = 2 * lines
    full = blocks * height
    count, packed = step_words(lines)
    bf16, f32 = jnp.bfloat16, jnp.float32
    return pl.pallas_call(
        functools.partial(fused_kernel, lines, rows, count, packed),
        out_shape=(
            jax.ShapeDtypeStruct(strip.shape, f32),
            jax.ShapeDtypeStruct((2, full, width), bf16),
        ),
        in_specs=[ANY, ANY, SMEM, SMEM],
        out_specs=(ANY, ANY),
        scratch_shapes=[
            pltpu.VMEM(strip.shape, f32),
            pltpu.VMEM(history.shape, bf16),
            pltpu.VMEM((coupling.shape[0], share), f32),
            pltpu.VMEM((blocks, 2, height, depth), bf16),
            pltpu.VMEM((blocks, 2, 2, height, share), bf16),
            pltpu.VMEM((blocks, 2, 2, height, share), bf16),
            pltpu.VMEM((blocks, 2, height, share), f32),
            pltpu.VMEM((blocks, 2, height, share), bf16),
            pltpu.VMEM((blocks, 2, height, share), bf16),
            pltpu.VMEM((2, full, share), f32),
            pltpu.VMEM((2, full, share), f32),
            pltpu.VMEM((2, full, share), f32),
            pltpu.VMEM((2, full, share), bf16),
            pltpu.VMEM((2, full, share), bf16),
            pltpu.VMEM((rows, 2, full, share), bf16),
            pltpu.VMEM((lines, 2, height, depth), bf16),
            pltpu.VMEM((lines, 2, height, depth), bf16),
            pltpu.VMEM((lines, 2, height, depth), bf16),
            pltpu.VMEM((lines + 1, 2, height, depth), bf16),
            pltpu.VMEM((lines - 1, 2, height, depth), f32),
            DMA((2, lines, CHUNKS)),
            DMA((lines, CHUNKS)),
            DMA((lines, CHUNKS)),
            DMA((lines, CHUNKS)),
            DMA((blocks, 4)),
            DMA((blocks, 4)),
            DMA((blocks, 4)),
            DMA((blocks, 4)),
            DMA((lines, 4)),
            DMA((lines, 4)),
            DMA((lines + 2,)),
            DMA((lines,)),
            DMA((lines,)),
            DMA((lines, CHUNKS)),
            DMA((lines + 1, CHUNKS)),
        ],
        compiler_params=pltpu.CompilerParams(
            collective_id=0, has_side_effects=True, vmem_limit_bytes=63 * 1024 * 1024
        ),
        name="group_updates",
    )(strip, history, coupling, dyson)


def widen_kernel(pieces, wide, later, out, later_out, rough, fine, passing, in_s, out_s, pass_s):
    size = wide.shape[1] // pieces

    def fetch(i):
        return pltpu.make_async_copy(wide.at[:, pl.ds(i * size, size)], rough.at[i], in_s.at[i])

    def put(i):
        return pltpu.make_async_copy(fine.at[i], out.at[:, pl.ds(i * size, size)], out_s.at[i])

    take = pltpu.make_async_copy(later, passing, pass_s.at[0])
    leave = pltpu.make_async_copy(passing, later_out, pass_s.at[1])
    for i in range(pieces):
        fetch(i).start()
    take.start()
    for i in range(pieces):
        fetch(i).wait()
        fine[i] = rough[i].astype(jnp.float32)
        put(i).start()
    take.wait()
    leave.start()
    for i in range(pieces):
        put(i).wait()
    leave.wait()


def widen(wide, later):
    pieces = 8
    piece = (pieces, 2, wide.shape[1] // pieces, wide.shape[2])
    return pl.pallas_call(
        functools.partial(widen_kernel, pieces),
        out_shape=(
            jax.ShapeDtypeStruct(wide.shape, jnp.float32),
            jax.ShapeDtypeStruct(later.shape, jnp.float32),
        ),
        in_specs=[ANY, ANY],
        out_specs=(ANY, ANY),
        scratch_shapes=[
            pltpu.VMEM(piece, jnp.bfloat16),
            pltpu.VMEM(piece, jnp.float32),
            pltpu.VMEM(later.shape, jnp.float32),
            DMA((pieces,)),
            DMA((pieces,)),
            DMA((2,)),
        ],
        compiler_params=pltpu.CompilerParams(vmem_limit_bytes=60 * 1024 * 1024),
        name="widen",
    )(wide, later)


def stacked_dyson(inverse, source):
    group_len = inverse.shape[1]
    matrix = TIME_STEP * jnp.concatenate(
        [
            jnp.concatenate([inverse[0], -inverse[1]], axis=1),
            jnp.concatenate([inverse[1], inverse[0]], axis=1),
        ],
        axis=0,
    )
    flat = source.reshape(2 * group_len, -1)
    solved = jnp.dot(
        matrix, flat, precision=lax.Precision.HIGHEST, preferred_element_type=jnp.float32
    )
    return solved.reshape(source.shape)


def shards(history, start_strip, coupling, dyson_inverse):
    row_count = lax.axis_size("row")
    col_count = lax.axis_size("col")
    row_index = lax.axis_index("row")
    col_index = lax.axis_index("col")
    strip_rows = start_strip.shape[1]
    strip_cols = start_strip.shape[2]
    group_rows = strip_rows * col_count
    tile_cols = history.shape[2]
    share_cols = tile_cols // row_count
    orbitals = coupling.shape[0]
    fits = (
        row_count == 4
        and col_count // 2 in ORDERS
        and col_count % 2 == 0
        and share_cols == 128
        and share_cols % orbitals == 0
        and strip_rows % (16 * CHUNKS) == 0
        and strip_rows % orbitals == 0
        and group_rows // orbitals == dyson_inverse.shape[2]
    )
    if fits:
        later_strip, wide = fused(
            start_strip, history, coupling, dyson_inverse, col_count // 2, row_count
        )
        return widen(wide, later_strip)
    sigma_first = self_energy(
        start_strip,
        orbital_weights(coupling, col_index * strip_rows, strip_rows),
        orbital_weights(coupling, row_index * strip_cols, strip_cols),
    ).astype(jnp.bfloat16)
    partial_first = complex_product(
        lax.all_gather(sigma_first, "col", axis=1, tiled=True), history
    )
    shares = lax.psum_scatter(partial_first, "row", scatter_dimension=2, tiled=True)
    solved_part = stacked_dyson(dyson_inverse[0], shares)
    sigma_second = self_energy(
        solved_part,
        orbital_weights(coupling, 0, group_rows),
        orbital_weights(coupling, col_index * tile_cols + row_index * share_cols, share_cols),
    ).astype(jnp.bfloat16)
    solved_sigma = stacked_dyson(
        dyson_inverse[1], sigma_second.astype(jnp.float32)
    ).astype(jnp.bfloat16)
    earlier = lax.all_gather(solved_part, "row", axis=2, tiled=True)
    tau = lax.all_gather(solved_sigma, "row", axis=2, tiled=True)
    partial_second = mirror_product(tau, history)
    later_strip = lax.psum_scatter(partial_second, "col", scatter_dimension=1, tiled=True)
    return (earlier, later_strip)


def solution(mesh):
    return jax.shard_map(
        shards,
        mesh=mesh,
        in_specs=(P(None, "row", "col"), P(None, "col", "row"), P(), P()),
        out_specs=(P(None, None, "col"), P(None, "col", "row")),
        check_vma=False,
    )
```

```python
import functools

import jax
import jax.numpy as jnp
from jax import lax
from jax.experimental import pallas as pl
from jax.experimental.pallas import tpu as pltpu
from jax.sharding import PartitionSpec as P

TIME_STEP = 0.15


def complex_product(first_pair, second_pair):
    real_out = jnp.dot(first_pair[0], second_pair[0], preferred_element_type=jnp.float32) - jnp.dot(
        first_pair[1], second_pair[1], preferred_element_type=jnp.float32
    )
    imag_out = jnp.dot(first_pair[0], second_pair[1], preferred_element_type=jnp.float32) + jnp.dot(
        first_pair[1], second_pair[0], preferred_element_type=jnp.float32
    )
    return jnp.stack([real_out, imag_out])


def mirror_product(sigma_pair, tile_pair):
    contract = (((1,), (1,)), ((), ()))
    real_real = lax.dot_general(
        sigma_pair[0], tile_pair[0], contract, preferred_element_type=jnp.float32
    )
    imag_imag = lax.dot_general(
        sigma_pair[1], tile_pair[1], contract, preferred_element_type=jnp.float32
    )
    real_imag = lax.dot_general(
        sigma_pair[0], tile_pair[1], contract, preferred_element_type=jnp.float32
    )
    imag_real = lax.dot_general(
        sigma_pair[1], tile_pair[0], contract, preferred_element_type=jnp.float32
    )
    return jnp.stack([-real_real - imag_imag, real_imag - imag_real])


def self_energy(green, row_weight, col_weight):
    magnitude = green[0] * green[0] + green[1] * green[1]
    factor = -(row_weight[:, None] * col_weight[None, :]) * magnitude
    return green * factor[None]


def orbital_weights(coupling, offset, count):
    orbitals = coupling.shape[0]
    position = (offset + jnp.arange(count, dtype=jnp.int32)) % orbitals
    one_hot = (position[:, None] == jnp.arange(orbitals, dtype=jnp.int32)[None, :]).astype(
        jnp.float32
    )
    return jnp.dot(
        one_hot, coupling, precision=lax.Precision.HIGHEST, preferred_element_type=jnp.float32
    )


MESH = pl.DeviceIdType.MESH
NN = (((1,), (0,)), ((), ()))
NT = (((1,), (1,)), ((), ()))
CHUNKS = 4
HEAD = 4
(
    RELAY,
    PRODUCT,
    SOLVE,
    UPDATE,
    SPREAD_TAU,
    GIVE,
    KEEP,
    CHAIN,
    SEND_NEAR,
    RELAY_NEAR,
    JOIN,
    NOTHING,
) = range(12)


def mm(x, y, dims):
    return lax.dot_general(x, y, dims, preferred_element_type=jnp.float32)


def remote(src, dst, send_sem, recv_sem, row, col):
    return pltpu.make_async_remote_copy(
        src_ref=src,
        dst_ref=dst,
        send_sem=send_sem,
        recv_sem=recv_sem,
        device_id=(row, col),
        device_id_type=MESH,
    )


ORDERS = {
    4: (
        (
            128, 129, 1280, 1281, 256, 272, 18, 1024, 17, 386, 16, 19, 144, 145,
            385, 1296, 32, 1297, 288, 304, 544, 35, 402, 560, 34, 33, 161, 656,
            160, 784, 1313, 1312, 51, 403, 320, 336, 50, 387, 576, 48, 49, 592,
            176, 177, 672, 1328, 800, 1329, 419, 528, 352, 368, 608, 624, 1072, 1056,
            688, 1152, 816, 1040, 512, 640, 1168, 768, 908, 909, 1184, 911, 1200, 910,
        ),
        (
            0, 145, 144, 32, 1, 2, 34, 35, 1296, 3, 33, 129, 128, 1280,
            160, 1281, 1297, 50, 161, 256, 51, 272, 385, 288, 48, 1313, 304, 1312,
            49, 177, 512, 402, 386, 528, 176, 320, 336, 576, 1329, 544, 419, 592,
            640, 1040, 1328, 403, 560, 672, 387, 800, 928, 768, 352, 368, 608, 930,
            624, 896, 1072, 1168, 656, 931, 688, 816, 899, 944, 945, 784, 1056, 897,
            898, 946, 1024, 914, 913, 916, 1200, 915, 947, 1152, 926, 920, 929, 1184,
            927, 925,
        ),
        (
            16, 160, 0, 50, 1, 49, 51, 161, 2, 3, 1313, 48, 128, 17,
            129, 176, 1312, 18, 1281, 1280, 177, 19, 256, 145, 144, 272, 512, 387,
            386, 528, 1296, 1329, 1297, 385, 1328, 640, 288, 304, 402, 320, 560, 336,
            403, 768, 896, 419, 576, 544, 897, 352, 368, 899, 898, 608, 592, 656,
            624, 1040, 784, 688, 1072, 912, 672, 1024, 1056, 913, 816, 1168, 914, 944,
            945, 915, 800, 946, 1152, 930, 1184, 928, 931, 1200, 947, 940, 942, 933,
            937, 943,
        ),
        (
            16, 0, 176, 32, 2, 1328, 1, 177, 3, 128, 129, 1280, 17, 1281,
            1329, 256, 18, 272, 386, 512, 19, 528, 144, 33, 34, 145, 640, 35,
            1296, 160, 768, 1297, 161, 385, 288, 304, 1312, 544, 402, 560, 1313, 1040,
            656, 320, 784, 336, 387, 1024, 592, 576, 1056, 419, 403, 352, 672, 368,
            1168, 800, 624, 608, 1072, 1184, 688, 1152, 816, 1200, 952, 954, 953, 955,
        ),
    ),
}

def step_words(lines):
    longest = max(len(steps) for steps in ORDERS[lines])
    longest += longest % 2
    packed = []
    for steps in ORDERS[lines]:
        codes = list(steps) + [NOTHING * 128] * (longest - len(steps))
        packed.append([codes[i] + 2048 * codes[i + 1] for i in range(0, longest, 2)])
    return longest, packed


def entry_barrier(row, q, core, lines, rows, wait):
    barrier = pltpu.get_barrier_semaphore()
    ends = jnp.minimum(q, 1) + jnp.minimum(lines - 1 - q, 1)
    if wait:
        pl.semaphore_wait(barrier, rows + ends)
        return

    def greet(to_row, to_col):
        pl.semaphore_signal(barrier, inc=1, device_id=(to_row, to_col), device_id_type=MESH)

    greet(row, 2 * q + 1 - core)
    for k in range(1, rows):
        greet(lax.rem(row + k, rows), 2 * q + core)

    @pl.when(q > 0)
    def _():
        greet(row, 2 * (q - 1) + core)

    @pl.when(q < lines - 1)
    def _():
        greet(row, 2 * (q + 1) + core)


def fused_kernel(
    lines, rows, count, packed, strip, history, coupling, inverse, later_out, wide,
    dyson, later, hist, weight, blocks, parts, first, keep, sums, joined, own, new, tau, source, near, taus,
    give, take, stage, land, held,
    hop_s, hop_r, pair_s, pair_r, sum_s, sum_r, tau_s, tau_r, near_s, near_r, local,
    give_s, give_r, chain_s, chain_r,
):
    row = lax.axis_index("row")
    col = lax.axis_index("col")
    q, core = lax.div(col, 2), lax.rem(col, 2)
    last = lines - 1
    height, depth = later.shape[1:]
    share = own.shape[2]
    orbitals = weight.shape[0]
    times = height // orbitals
    total = times * 2 * lines
    piece = height // CHUNKS
    beside = row + 1 - 2 * lax.rem(row, 2)
    across = lax.rem(row + 2, 4)
    direct = [beside, across]
    bf16 = jnp.bfloat16

    def head_start(at):
        return lax.div(at * CHUNKS, HEAD)

    def span(j):
        return pl.ds(pl.multiple_of(j * height, height), height)

    def double(m):
        return pl.ds(pl.multiple_of(2 * m * height, 2 * height), 2 * height)

    def cut(k):
        return pl.ds(pl.multiple_of(k * piece, piece), piece)

    def columns(r):
        return pl.ds(pl.multiple_of(r * share, share), share)

    def slab(n):
        return pl.ds(pl.multiple_of(n * orbitals, orbitals), orbitals)

    def hop(way, m, k):
        block = blocks.at[2 * m + core, :, cut(k)]
        to = 2 * (q + 1 - 2 * way) + core
        return remote(block, block, hop_s.at[way, m], hop_r.at[m, k], row, to)

    def settle(ref, send_sem, recv_sem):
        return remote(ref, ref, send_sem, recv_sem, row, 2 * q + 1 - core)

    def pair(m, k):
        block = blocks.at[2 * m + core, :, cut(k)]
        return remote(block, block, pair_s.at[0], pair_r.at[m], row, 2 * q + 1 - core)

    def send_parts(j, k):
        return remote(
            parts.at[j, k], first.at[j, k], sum_s.at[k], sum_r.at[j, k], direct[k], col
        )

    def send_joined(j, k):
        return remote(
            sums.at[j, k], joined.at[j, k], sum_s.at[2 + k], sum_r.at[j, 2 + k],
            direct[1 - k], col,
        )

    def send_tau(j, k):
        block = taus.at[row, :, span(j)]
        return remote(block, block, tau_s.at[k], tau_r.at[j, k], direct[k], col)

    def relay_tau(j, k):
        block = taus.at[direct[k], k, span(j)]
        return remote(block, block, tau_s.at[2 + k], tau_r.at[j, 2 + k], direct[1 - k], col)

    def send_near(m, k):
        return remote(
            near.at[:, double(m)],
            wide.at[:, double(m), columns(row)],
            near_s.at[k],
            near_r.at[m, k],
            direct[k],
            col,
        )

    def relay_near(m, k):
        block = wide.at[k, double(m), columns(direct[k])]
        return remote(block, block, near_s.at[2 + k], near_r.at[m, 2 + k], direct[1 - k], col)

    def own_near(m):
        return pltpu.make_async_copy(
            near.at[:, double(m)], wide.at[:, double(m), columns(row)], local.at[m]
        )

    def swap(d):
        return remote(give.at[d], take.at[d], give_s.at[0], give_r.at[d], row, 2 * q + 1 - core)

    def chain(way, d, k):
        to = q + 1 - 2 * way
        slot = jnp.where(jnp.logical_and(d == to, way == 1), lines, d)
        return remote(
            stage.at[d, :, cut(k)],
            land.at[slot, :, cut(k)],
            chain_s.at[0],
            chain_r.at[slot, k],
            row,
            2 * to + core,
        )

    def chain_on(d, k):
        @pl.when(d > q)
        def _():
            chain(0, d, k).start()

        @pl.when(d < q)
        def _():
            chain(1, d, k).start()

    def update(acc, src, group, low, n, j):
        def add(i, c):
            at = low + i
            real, imag = acc[0, slab(at), :], acc[1, slab(at), :]
            for t in range(times):
                m = j * times + t
                dr, di = dyson[group, 0, at, m], dyson[group, 1, at, m]
                sr = src[0, slab(m), :].astype(jnp.float32)
                si = src[1, slab(m), :].astype(jnp.float32)
                real += dr * sr - di * si
                imag += dr * si + di * sr
            acc[0, slab(at), :] = real
            acc[1, slab(at), :] = imag
            return c

        lax.fori_loop(0, n, add, 0)

    def op_relay(m, k):
        hop(0, m, k).wait_recv()

        @pl.when(jnp.logical_and(m < q, q < last))
        def _():
            hop(0, m, k).start()

        @pl.when(jnp.logical_and(m > q, q > 0))
        def _():
            hop(1, m, k).start()

        pair(m, k).start()

        @pl.when(jnp.logical_and(m == q - 1, k == CHUNKS - 1))
        def _():
            rest()

    def rest():
        for x in range(CHUNKS):

            @pl.when(jnp.logical_and(q < last, jnp.logical_and(q > 0, x >= head_start(q))))
            def _():
                hop(0, q, x).start()

    def op_product(m, other):
        @pl.when(other == 1)
        def _():
            block = blocks.at[2 * m + 1 - core]
            settle(block, pair_s.at[0], pair_r.at[m]).wait_recv()

        j = 2 * m + core + other - 2 * core * other
        real = mm(blocks[j, 0], hist[0], NN) - mm(blocks[j, 1], hist[1], NN)
        imag = mm(blocks[j, 0], hist[1], NN) + mm(blocks[j, 1], hist[0], NN)
        for r in range(rows):

            @pl.when(row == r)
            def _():
                mine, near_x, near_y, far = [
                    slice(x * share, (x + 1) * share) for x in (r, r ^ 1, r ^ 2, r ^ 3)
                ]
                parts[j, 0, 0] = real[:, near_x].astype(bf16)
                parts[j, 0, 1] = real[:, far].astype(bf16)
                parts[j, 1, 0] = imag[:, near_y].astype(bf16)
                parts[j, 1, 1] = imag[:, far].astype(bf16)
                keep[j, 0] = real[:, near_y]
                keep[j, 1] = imag[:, near_x]
                own[0, span(j), :] = real[:, mine]
                own[1, span(j), :] = imag[:, mine]

        for k in (0, 1):
            send_parts(j, k).start()

    def op_join(m, other):
        j = 2 * m + core + other - 2 * core * other
        for k in (0, 1):
            send_parts(j, k).wait_recv()
            sums[j, k] = (keep[j, k] + first[j, k, 1].astype(jnp.float32)).astype(bf16)
        for k in (0, 1):
            send_joined(j, k).start()

    def op_solve(j):
        at = span(j)
        for p in (0, 1):
            send_joined(j, p).wait_recv()
            others = first[j, p, 0].astype(jnp.float32) + joined[j, p].astype(jnp.float32)
            own[p, at, :] = TIME_STEP * (own[p, at, :] + others)

        @pl.when(lax.rem(j, 2) == 1)
        def _():
            update(new, own, 0, j * times, times, j - 1)

        update(new, own, 0, j * times, times, j)

        def sigma(i, c):
            rows_at = slab(j * times + i)
            real, imag = new[0, rows_at, :], new[1, rows_at, :]
            near[0, rows_at, :] = real.astype(bf16)
            near[1, rows_at, :] = imag.astype(bf16)
            factor = weight[...] * (real * real + imag * imag)
            source[0, rows_at, :] = (real * factor).astype(bf16)
            source[1, rows_at, :] = (imag * factor).astype(bf16)
            return c

        lax.fori_loop(0, times, sigma, 0)

        @pl.when(lax.rem(j, 2) == 1)
        def _():
            update(tau, source, 1, j * times, times, j - 1)

        update(tau, source, 1, j * times, times, j)
        for p in (0, 1):
            taus[row, p, at, :] = (TIME_STEP * tau[p, at, :]).astype(bf16)
        for k in (0, 1):
            send_tau(j, k).start()

    def op_update(m, later_m):
        def both(half, c):
            update(new, own, 0, 2 * times * later_m, 2 * times, 2 * m + half)
            update(tau, source, 1, 2 * times * later_m, 2 * times, 2 * m + half)
            return c

        lax.fori_loop(0, 2, both, 0)

    def op_spread_tau(j):
        for k in (0, 1):
            send_tau(j, k).wait_recv()
        for k in (0, 1):
            relay_tau(j, k).start()

    def second(j):
        for k in (0, 1):
            relay_tau(j, k).wait_recv()
        at = span(j)
        real_in = jnp.concatenate([taus[r, 0, at, :] for r in range(rows)], axis=1)
        imag_in = jnp.concatenate([taus[r, 1, at, :] for r in range(rows)], axis=1)
        real = -mm(real_in, hist[0], NT) - mm(imag_in, hist[1], NT)
        imag = mm(real_in, hist[1], NT) - mm(imag_in, hist[0], NT)
        return real, imag

    def held_at(d):
        return d - jnp.where(d > q, 1, 0)

    def op_second(d, keep):
        pair_sums = second(2 * d + core + (1 - keep) * (1 - 2 * core))

        @pl.when(keep == 0)
        def _():
            for p in (0, 1):
                give[d, p] = pair_sums[p].astype(bf16)
            swap(d).start()

        @pl.when(keep == 1)
        def _():
            swap(d).wait_recv()
            begins = jnp.logical_or(
                jnp.logical_and(d < q, q == last), jnp.logical_and(d > q, q == 0)
            )

            @pl.when(d == q)
            def _():
                for p in (0, 1):
                    later[p] = pair_sums[p] + take[d, p].astype(jnp.float32)

            @pl.when(begins)
            def _():
                for p in (0, 1):
                    value = pair_sums[p] + take[d, p].astype(jnp.float32)
                    stage[d, p] = value.astype(bf16)
                for k in range(CHUNKS):
                    chain_on(d, k)

            @pl.when(jnp.logical_and(d != q, jnp.logical_not(begins)))
            def _():
                for p in (0, 1):
                    held[held_at(d), p] = pair_sums[p] + take[d, p].astype(jnp.float32)

    def op_chain(d, b):
        ends, way, k = lax.div(b, 2 * CHUNKS), lax.rem(lax.div(b, CHUNKS), 2), lax.rem(b, CHUNKS)
        at = cut(k)
        slot = jnp.where(way == 1, lines, d)
        pltpu.make_async_remote_copy(
            src_ref=stage.at[d, :, at],
            dst_ref=land.at[slot, :, at],
            send_sem=chain_s.at[0],
            recv_sem=chain_r.at[slot, k],
            device_id=(row, 2 * q + 1 - core),
            device_id_type=MESH,
        ).wait_recv()

        @pl.when(d == q)
        def _():
            for p in (0, 1):
                later[p, at, :] += land[slot, p, at, :].astype(jnp.float32)

            @pl.when(ends == 1)
            def _():
                pltpu.make_async_copy(
                    later.at[:, at], later_out.at[:, at], local.at[lines]
                ).start()

        @pl.when(d != q)
        def _():
            for p in (0, 1):
                value = held[held_at(d), p, at, :] + land[slot, p, at, :].astype(jnp.float32)
                stage[d, p, at, :] = value.astype(bf16)
            chain_on(d, k)

    def op_send_near(m):
        own_near(m).start()
        for k in (0, 1):
            send_near(m, k).start()

    def op_relay_near(m):
        for k in (0, 1):
            send_near(m, k).wait_recv()
        for k in (0, 1):
            relay_near(m, k).start()

    load_hist = pltpu.make_async_copy(history, hist, local.at[lines])
    load_strip = pltpu.make_async_copy(strip, later, local.at[lines + 1])
    load_dyson = pltpu.make_async_copy(inverse, dyson, local.at[lines + 2])
    load_strip.start()
    load_hist.start()
    load_dyson.start()
    entry_barrier(row, q, core, lines, rows, False)
    place_row = lax.broadcasted_iota(jnp.int32, (orbitals, share), 0)
    place_col = lax.rem(lax.broadcasted_iota(jnp.int32, (orbitals, share), 1), orbitals)
    down = jnp.zeros((orbitals, share), jnp.float32)
    along = jnp.zeros((orbitals, share), jnp.float32)
    for a in range(orbitals):
        down = jnp.where(place_row == a, coupling[a], down)
        along = jnp.where(place_col == a, coupling[a], along)
    weight[...] = -(down * along)
    load_strip.wait()

    def fill(i, c):
        at = slab(i)
        scale = jnp.concatenate([weight[...]] * (depth // share), axis=1)
        real, imag = later[0, at, :], later[1, at, :]
        factor = scale * (real * real + imag * imag)
        blocks[col, 0, at, :] = (real * factor).astype(bf16)
        blocks[col, 1, at, :] = (imag * factor).astype(bf16)
        return c

    lax.fori_loop(0, times, fill, 0)
    entry_barrier(row, q, core, lines, rows, True)

    for x in range(CHUNKS):

        @pl.when(jnp.logical_and(q < last, jnp.logical_or(q == 0, x < head_start(q))))
        def _():
            hop(0, q, x).start()

    for x in range(CHUNKS):

        @pl.when(q > 0)
        def _():
            hop(1, q, x).start()

    for x in range(CHUNKS):
        pair(q, x).start()

    def clear(n, c):
        for p in (0, 1):
            new[p, slab(n), :] = jnp.zeros((orbitals, share), jnp.float32)
            tau[p, slab(n), :] = jnp.zeros((orbitals, share), jnp.float32)
        return c

    lax.fori_loop(0, total, clear, 0)
    load_hist.wait()
    load_dyson.wait()

    words = []
    for w in range(count // 2):
        word = jnp.int32(packed[last][w])
        for x in range(last):
            word = jnp.where(q == x, jnp.int32(packed[x][w]), word)
        words.append(word)

    def step(i, c):
        which, place = lax.div(i, 2), lax.rem(i, 2)
        word = words[0]
        for w in range(1, len(words)):
            word = jnp.where(which == w, words[w], word)
        code = jnp.where(place == 1, lax.div(word, 2048), lax.rem(word, 2048))
        kind, a, b = lax.div(code, 128), lax.rem(lax.div(code, 16), 8), lax.rem(code, 16)

        @pl.when(kind == RELAY)
        def _():
            op_relay(a, b)

        @pl.when(kind == PRODUCT)
        def _():
            op_product(a, b)

        @pl.when(kind == JOIN)
        def _():
            op_join(a, b)

        @pl.when(kind == SOLVE)
        def _():
            op_solve(a)

        @pl.when(kind == UPDATE)
        def _():
            op_update(a, b)

        @pl.when(kind == SPREAD_TAU)
        def _():
            op_spread_tau(a)

        @pl.when(jnp.logical_or(kind == GIVE, kind == KEEP))
        def _():
            op_second(a, kind - GIVE)

        @pl.when(kind == CHAIN)
        def _():
            op_chain(a, b)

        @pl.when(kind == SEND_NEAR)
        def _():
            op_send_near(a)

        @pl.when(kind == RELAY_NEAR)
        def _():
            op_relay_near(a)

        return c

    lax.fori_loop(0, count, step, 0)

    def drain(m, c):
        block = blocks.at[2 * m + core]

        @pl.when(jnp.logical_and(m <= q, q < last))
        def _():
            settle(block, hop_s.at[0, m], hop_r.at[m, 0]).wait_send()

        @pl.when(jnp.logical_and(m >= q, q > 0))
        def _():
            settle(block, hop_s.at[1, m], hop_r.at[m, 0]).wait_send()

        own_near(m).wait()
        for k in (0, 1):
            relay_near(m, k).wait_recv()
        return c

    lax.fori_loop(0, lines, drain, 0)
    settle(blocks.at[pl.ds(0, lines)], pair_s.at[0], pair_r.at[0]).wait_send()
    for k in (0, 1):
        settle(parts.at[:, k], sum_s.at[k], sum_r.at[0, 0]).wait_send()
        settle(sums.at[:, k], sum_s.at[2 + k], sum_r.at[0, 0]).wait_send()
        settle(taus.at[k], tau_s.at[k], tau_r.at[0, 0]).wait_send()
        settle(taus.at[0, k], tau_s.at[2 + k], tau_r.at[0, 0]).wait_send()
        settle(near, near_s.at[k], near_r.at[0, 0]).wait_send()
        settle(near.at[k], near_s.at[2 + k], near_r.at[0, 0]).wait_send()
    settle(give, give_s.at[0], give_r.at[0]).wait_send()
    settle(stage.at[pl.ds(0, last)], chain_s.at[0], chain_r.at[0, 0]).wait_send()
    pltpu.make_async_copy(later, later_out, local.at[lines]).wait()


VMEM = pl.BlockSpec(memory_space=pltpu.VMEM)
ANY = pl.BlockSpec(memory_space=pl.ANY)
SMEM = pl.BlockSpec(memory_space=pltpu.SMEM)
DMA = pltpu.SemaphoreType.DMA


def fused(strip, history, coupling, dyson, lines, rows):
    height, depth = strip.shape[1:]
    width = history.shape[2]
    share = width // rows
    blocks = 2 * lines
    full = blocks * height
    count, packed = step_words(lines)
    bf16, f32 = jnp.bfloat16, jnp.float32
    return pl.pallas_call(
        functools.partial(fused_kernel, lines, rows, count, packed),
        out_shape=(
            jax.ShapeDtypeStruct(strip.shape, f32),
            jax.ShapeDtypeStruct((2, full, width), bf16),
        ),
        in_specs=[ANY, ANY, SMEM, ANY],
        out_specs=(ANY, ANY),
        scratch_shapes=[
            pltpu.SMEM(dyson.shape, f32),
            pltpu.VMEM(strip.shape, f32),
            pltpu.VMEM(history.shape, bf16),
            pltpu.VMEM((coupling.shape[0], share), f32),
            pltpu.VMEM((blocks, 2, height, depth), bf16),
            pltpu.VMEM((blocks, 2, 2, height, share), bf16),
            pltpu.VMEM((blocks, 2, 2, height, share), bf16),
            pltpu.VMEM((blocks, 2, height, share), f32),
            pltpu.VMEM((blocks, 2, height, share), bf16),
            pltpu.VMEM((blocks, 2, height, share), bf16),
            pltpu.VMEM((2, full, share), f32),
            pltpu.VMEM((2, full, share), f32),
            pltpu.VMEM((2, full, share), f32),
            pltpu.VMEM((2, full, share), bf16),
            pltpu.VMEM((2, full, share), bf16),
            pltpu.VMEM((rows, 2, full, share), bf16),
            pltpu.VMEM((lines, 2, height, depth), bf16),
            pltpu.VMEM((lines, 2, height, depth), bf16),
            pltpu.VMEM((lines, 2, height, depth), bf16),
            pltpu.VMEM((lines + 1, 2, height, depth), bf16),
            pltpu.VMEM((lines - 1, 2, height, depth), f32),
            DMA((2, lines)),
            DMA((lines, CHUNKS)),
            DMA((1,)),
            DMA((lines,)),
            DMA((4,)),
            DMA((blocks, 4)),
            DMA((4,)),
            DMA((blocks, 4)),
            DMA((4,)),
            DMA((lines, 4)),
            DMA((lines + 3,)),
            DMA((1,)),
            DMA((lines,)),
            DMA((1,)),
            DMA((lines + 1, CHUNKS)),
        ],
        compiler_params=pltpu.CompilerParams(
            collective_id=0, has_side_effects=True, vmem_limit_bytes=63 * 1024 * 1024
        ),
        name="group_updates",
    )(strip, history, coupling, dyson)


def widen_kernel(pieces, wide, later, out, later_out, rough, fine, passing, in_s, out_s, pass_s):
    size = wide.shape[1] // pieces

    def fetch(i):
        return pltpu.make_async_copy(wide.at[:, pl.ds(i * size, size)], rough.at[i], in_s.at[i])

    def put(i):
        return pltpu.make_async_copy(fine.at[i], out.at[:, pl.ds(i * size, size)], out_s.at[i])

    take = pltpu.make_async_copy(later, passing, pass_s.at[0])
    leave = pltpu.make_async_copy(passing, later_out, pass_s.at[1])
    for i in range(pieces):
        fetch(i).start()
    take.start()
    for i in range(pieces):
        fetch(i).wait()
        fine[i] = rough[i].astype(jnp.float32)
        put(i).start()
    take.wait()
    leave.start()
    for i in range(pieces):
        put(i).wait()
    leave.wait()


def widen(wide, later):
    pieces = 8
    piece = (pieces, 2, wide.shape[1] // pieces, wide.shape[2])
    return pl.pallas_call(
        functools.partial(widen_kernel, pieces),
        out_shape=(
            jax.ShapeDtypeStruct(wide.shape, jnp.float32),
            jax.ShapeDtypeStruct(later.shape, jnp.float32),
        ),
        in_specs=[ANY, ANY],
        out_specs=(ANY, ANY),
        scratch_shapes=[
            pltpu.VMEM(piece, jnp.bfloat16),
            pltpu.VMEM(piece, jnp.float32),
            pltpu.VMEM(later.shape, jnp.float32),
            DMA((pieces,)),
            DMA((pieces,)),
            DMA((2,)),
        ],
        compiler_params=pltpu.CompilerParams(vmem_limit_bytes=60 * 1024 * 1024),
        name="widen",
    )(wide, later)


def stacked_dyson(inverse, source):
    group_len = inverse.shape[1]
    matrix = TIME_STEP * jnp.concatenate(
        [
            jnp.concatenate([inverse[0], -inverse[1]], axis=1),
            jnp.concatenate([inverse[1], inverse[0]], axis=1),
        ],
        axis=0,
    )
    flat = source.reshape(2 * group_len, -1)
    solved = jnp.dot(
        matrix, flat, precision=lax.Precision.HIGHEST, preferred_element_type=jnp.float32
    )
    return solved.reshape(source.shape)


def shards(history, start_strip, coupling, dyson_inverse):
    row_count = lax.axis_size("row")
    col_count = lax.axis_size("col")
    row_index = lax.axis_index("row")
    col_index = lax.axis_index("col")
    strip_rows = start_strip.shape[1]
    strip_cols = start_strip.shape[2]
    group_rows = strip_rows * col_count
    tile_cols = history.shape[2]
    share_cols = tile_cols // row_count
    orbitals = coupling.shape[0]
    fits = (
        row_count == 4
        and col_count // 2 in ORDERS
        and col_count % 2 == 0
        and share_cols == 128
        and share_cols % orbitals == 0
        and strip_rows % (16 * CHUNKS) == 0
        and strip_rows % orbitals == 0
        and group_rows // orbitals == dyson_inverse.shape[2]
    )
    if fits:
        later_strip, wide = fused(
            start_strip, history, coupling, dyson_inverse, col_count // 2, row_count
        )
        return widen(wide, later_strip)
    sigma_first = self_energy(
        start_strip,
        orbital_weights(coupling, col_index * strip_rows, strip_rows),
        orbital_weights(coupling, row_index * strip_cols, strip_cols),
    ).astype(jnp.bfloat16)
    partial_first = complex_product(
        lax.all_gather(sigma_first, "col", axis=1, tiled=True), history
    )
    shares = lax.psum_scatter(partial_first, "row", scatter_dimension=2, tiled=True)
    solved_part = stacked_dyson(dyson_inverse[0], shares)
    sigma_second = self_energy(
        solved_part,
        orbital_weights(coupling, 0, group_rows),
        orbital_weights(coupling, col_index * tile_cols + row_index * share_cols, share_cols),
    ).astype(jnp.bfloat16)
    solved_sigma = stacked_dyson(
        dyson_inverse[1], sigma_second.astype(jnp.float32)
    ).astype(jnp.bfloat16)
    earlier = lax.all_gather(solved_part, "row", axis=2, tiled=True)
    tau = lax.all_gather(solved_sigma, "row", axis=2, tiled=True)
    partial_second = mirror_product(tau, history)
    later_strip = lax.psum_scatter(partial_second, "col", scatter_dimension=1, tiled=True)
    return (earlier, later_strip)


def solution(mesh):
    return jax.shard_map(
        shards,
        mesh=mesh,
        in_specs=(P(None, "row", "col"), P(None, "col", "row"), P(), P()),
        out_specs=(P(None, None, "col"), P(None, "col", "row")),
        check_vma=False,
    )
```

```python
import functools

import jax
import jax.numpy as jnp
from jax import lax
from jax.experimental import pallas as pl
from jax.experimental.pallas import tpu as pltpu
from jax.sharding import PartitionSpec as P

TIME_STEP = 0.15


def complex_product(first_pair, second_pair):
    real_out = jnp.dot(first_pair[0], second_pair[0], preferred_element_type=jnp.float32) - jnp.dot(
        first_pair[1], second_pair[1], preferred_element_type=jnp.float32
    )
    imag_out = jnp.dot(first_pair[0], second_pair[1], preferred_element_type=jnp.float32) + jnp.dot(
        first_pair[1], second_pair[0], preferred_element_type=jnp.float32
    )
    return jnp.stack([real_out, imag_out])


def mirror_product(sigma_pair, tile_pair):
    contract = (((1,), (1,)), ((), ()))
    real_real = lax.dot_general(
        sigma_pair[0], tile_pair[0], contract, preferred_element_type=jnp.float32
    )
    imag_imag = lax.dot_general(
        sigma_pair[1], tile_pair[1], contract, preferred_element_type=jnp.float32
    )
    real_imag = lax.dot_general(
        sigma_pair[0], tile_pair[1], contract, preferred_element_type=jnp.float32
    )
    imag_real = lax.dot_general(
        sigma_pair[1], tile_pair[0], contract, preferred_element_type=jnp.float32
    )
    return jnp.stack([-real_real - imag_imag, real_imag - imag_real])


def self_energy(green, row_weight, col_weight):
    magnitude = green[0] * green[0] + green[1] * green[1]
    factor = -(row_weight[:, None] * col_weight[None, :]) * magnitude
    return green * factor[None]


def orbital_weights(coupling, offset, count):
    orbitals = coupling.shape[0]
    position = (offset + jnp.arange(count, dtype=jnp.int32)) % orbitals
    one_hot = (position[:, None] == jnp.arange(orbitals, dtype=jnp.int32)[None, :]).astype(
        jnp.float32
    )
    return jnp.dot(
        one_hot, coupling, precision=lax.Precision.HIGHEST, preferred_element_type=jnp.float32
    )


MESH = pl.DeviceIdType.MESH
NN = (((1,), (0,)), ((), ()))
NT = (((1,), (1,)), ((), ()))
CHUNKS = 8
HEAD = 4
LINKS = 4
RELAY, UPDATE, PRODUCT, JOIN, SOLVE, SPREAD_TAU, SECOND, SEND_NEAR, RELAY_NEAR, NOTHING = (
    64,
    96,
    112,
    128,
    144,
    152,
    160,
    168,
    172,
    176,
)


def mm(x, y, dims):
    return lax.dot_general(x, y, dims, preferred_element_type=jnp.float32)


def remote(src, dst, send_sem, recv_sem, row, col):
    return pltpu.make_async_remote_copy(
        src_ref=src,
        dst_ref=dst,
        send_sem=send_sem,
        recv_sem=recv_sem,
        device_id=(row, col),
        device_id_type=MESH,
    )


ORDERS = {
    4: (
        (
            113, 112, 114, 115, 128, 129, 130, 131, 144, 145, 72, 97, 152, 118, 116, 153,
            134, 73, 117, 119, 133, 132, 135, 168, 99, 146, 147, 80, 98, 120, 154, 102,
            155, 122, 136, 81, 121, 123, 161, 138, 165, 137, 139, 103, 148, 149, 88, 156,
            126, 157, 89, 125, 127, 162, 124, 166, 141, 143, 142, 140, 107, 150, 151, 158,
            160, 159, 170, 172, 163, 171, 167, 169, 174, 164, 175, 173, 14, 12, 15, 13,
        ),
        (
            116, 119, 64, 117, 65, 118, 132, 66, 67, 135, 133, 134, 112, 114, 68, 80,
            122, 69, 128, 130, 70, 120, 71, 113, 115, 81, 121, 129, 131, 136, 138, 137,
            123, 144, 145, 88, 97, 139, 124, 126, 146, 152, 153, 98, 147, 103, 154, 142,
            89, 125, 127, 140, 155, 102, 148, 149, 99, 161, 156, 141, 143, 107, 157, 150,
            151, 162, 165, 16, 158, 159, 17, 166, 170, 32, 160, 164, 169, 1, 163, 19,
            34, 3, 174, 167, 168, 35, 2, 18, 48, 171, 172, 49, 0, 173, 175, 28,
            50, 30, 51, 29, 33, 31,
        ),
        (
            120, 122, 121, 138, 123, 136, 137, 64, 65, 139, 66, 67, 112, 88, 124, 68,
            128, 89, 69, 140, 114, 127, 70, 130, 71, 113, 73, 72, 115, 143, 126, 129,
            75, 74, 116, 131, 142, 132, 77, 118, 144, 78, 76, 79, 117, 119, 145, 134,
            97, 135, 133, 152, 98, 153, 146, 147, 99, 154, 102, 155, 125, 148, 160, 103,
            141, 164, 1, 156, 149, 0, 107, 150, 157, 161, 3, 158, 151, 165, 2, 162,
            159, 171, 16, 169, 163, 166, 168, 32, 170, 17, 167, 173, 18, 19, 48, 35,
            172, 49, 175, 50, 51, 34, 37, 46, 174, 47, 44, 41,
        ),
        (
            125, 126, 124, 141, 127, 140, 81, 83, 80, 82, 120, 143, 122, 142, 136, 66,
            65, 64, 67, 138, 112, 128, 68, 69, 114, 70, 71, 113, 115, 129, 131, 130,
            144, 145, 97, 74, 152, 73, 77, 72, 153, 75, 118, 116, 76, 78, 160, 79,
            117, 119, 134, 164, 133, 84, 132, 85, 86, 135, 87, 121, 123, 146, 147, 102,
            139, 154, 155, 137, 168, 98, 161, 148, 165, 149, 172, 107, 156, 103, 157, 99,
            150, 151, 162, 171, 166, 158, 159, 175, 169, 170, 163, 167, 56, 173, 58, 174,
            57, 59,
        ),
    ),
}

def step_words(lines):
    longest = max(len(steps) for steps in ORDERS[lines])
    longest += -longest % 4
    packed = []
    for steps in ORDERS[lines]:
        codes = list(steps) + [NOTHING] * (longest - len(steps))
        words = []
        for i in range(0, longest, 4):
            word = sum(code << (8 * k) for k, code in enumerate(codes[i : i + 4]))
            words.append(word - (1 << 32) * (word >> 31))
        packed.append(words)
    return longest, packed


def entry_barrier(row, q, core, lines, rows, wait):
    barrier = pltpu.get_barrier_semaphore()
    ends = jnp.minimum(q, 1) + jnp.minimum(lines - 1 - q, 1)
    if wait:
        pl.semaphore_wait(barrier, rows + ends)
        return

    def greet(to_row, to_col):
        pl.semaphore_signal(barrier, inc=1, device_id=(to_row, to_col), device_id_type=MESH)

    greet(row, 2 * q + 1 - core)
    for k in range(1, rows):
        greet(lax.rem(row + k, rows), 2 * q + core)

    @pl.when(q > 0)
    def _():
        greet(row, 2 * (q - 1) + core)

    @pl.when(q < lines - 1)
    def _():
        greet(row, 2 * (q + 1) + core)


def fused_kernel(
    lines, rows, count, packed, strip, history, coupling, inverse, later_out, wide,
    dyson, later, hist, weight, blocks, parts, first, keep, sums, joined, own, new, tau, source, near, taus,
    give, take, stage, land, held,
    hop_s, hop_r, pair_s, pair_r, sum_s, sum_r, tau_s, tau_r, near_s, near_r, local,
    give_s, give_r, chain_s, chain_r,
):
    row = lax.axis_index("row")
    col = lax.axis_index("col")
    q, core = lax.div(col, 2), lax.rem(col, 2)
    last = lines - 1
    height, depth = later.shape[1:]
    share = own.shape[2]
    orbitals = weight.shape[0]
    times = height // orbitals
    total = times * 2 * lines
    piece = height // CHUNKS
    length = height // LINKS
    half = height // 2
    beside = row + 1 - 2 * lax.rem(row, 2)
    across = lax.rem(row + 2, 4)
    direct = [beside, across]
    bf16 = jnp.bfloat16

    def head_start(at):
        return lax.div(at * CHUNKS, HEAD)

    def span(j):
        return pl.ds(pl.multiple_of(j * height, height), height)

    def double(m):
        return pl.ds(pl.multiple_of(2 * m * height, 2 * height), 2 * height)

    def cut(k):
        return pl.ds(pl.multiple_of(k * piece, piece), piece)

    def link(k):
        return pl.ds(pl.multiple_of(k * length, length), length)

    def side(h):
        return pl.ds(pl.multiple_of(h * half, half), half)

    def columns(r):
        return pl.ds(pl.multiple_of(r * share, share), share)

    def slab(n):
        return pl.ds(pl.multiple_of(n * orbitals, orbitals), orbitals)

    def hop(way, m, k):
        block = blocks.at[2 * m + core, :, cut(k)]
        to = 2 * (q + 1 - 2 * way) + core
        return remote(block, block, hop_s.at[way, m], hop_r.at[m, k], row, to)

    def settle(ref, send_sem, recv_sem):
        return remote(ref, ref, send_sem, recv_sem, row, 2 * q + 1 - core)

    def pair(m, k):
        block = blocks.at[2 * m + core, :, cut(k)]
        there = pair_r.at[m, k // (CHUNKS // 2)]
        return remote(block, block, pair_s.at[0], there, row, 2 * q + 1 - core)

    def send_parts(j, h, k):
        return remote(
            parts.at[j, k, :, side(h)],
            first.at[j, k, :, side(h)],
            sum_s.at[k],
            sum_r.at[j, h, k],
            direct[k],
            col,
        )

    def send_joined(j, h, k):
        return remote(
            sums.at[j, k, side(h)],
            joined.at[j, k, side(h)],
            sum_s.at[2 + k],
            sum_r.at[j, h, 2 + k],
            direct[1 - k],
            col,
        )

    def send_tau(j, k):
        block = taus.at[row, :, span(j)]
        return remote(block, block, tau_s.at[k], tau_r.at[j, k], direct[k], col)

    def relay_tau(j, k):
        block = taus.at[direct[k], k, span(j)]
        return remote(block, block, tau_s.at[2 + k], tau_r.at[j, 2 + k], direct[1 - k], col)

    def send_near(m, k):
        return remote(
            near.at[:, double(m)],
            wide.at[:, double(m), columns(row)],
            near_s.at[k],
            near_r.at[m, k],
            direct[k],
            col,
        )

    def relay_near(m, k):
        block = wide.at[k, double(m), columns(direct[k])]
        return remote(block, block, near_s.at[2 + k], near_r.at[m, 2 + k], direct[1 - k], col)

    def own_near(m):
        return pltpu.make_async_copy(
            near.at[:, double(m)], wide.at[:, double(m), columns(row)], local.at[m]
        )

    def swap(d):
        return remote(give.at[d], take.at[d], give_s.at[0], give_r.at[d], row, 2 * q + 1 - core)

    def chain(way, d, k):
        to = q + 1 - 2 * way
        slot = jnp.where(jnp.logical_and(d == to, way == 1), lines, d)
        return remote(
            stage.at[d, :, link(k)],
            land.at[slot, :, link(k)],
            chain_s.at[0],
            chain_r.at[slot, k],
            row,
            2 * to + core,
        )

    def chain_on(d, k):
        @pl.when(d > q)
        def _():
            chain(0, d, k).start()

        @pl.when(d < q)
        def _():
            chain(1, d, k).start()

    def update(acc, src, group, low, n, j):
        def add(i, c):
            lines_at = [low + 2 * i, low + 2 * i + 1]
            sums3 = []
            for at in lines_at:
                real, imag = acc[0, slab(at), :], acc[1, slab(at), :]
                sums3.append([real, jnp.zeros_like(real), real + imag])
            for t in range(times):
                m = j * times + t
                planes = [src[p, slab(m), :] for p in (0, 1, 2)]
                for at, three in zip(lines_at, sums3):
                    dr, di = dyson[group, 0, at, m], dyson[group, 1, at, m]
                    for p, d in enumerate((dr, di, dr + di)):
                        three[p] = three[p] + d * planes[p]
            for at, three in zip(lines_at, sums3):
                acc[0, slab(at), :] = three[0] - three[1]
                acc[1, slab(at), :] = three[2] - three[0] - three[1]
            return c

        lax.fori_loop(0, n // 2, add, 0)

    def op_relay(m, b):
        @pl.when(m < q)
        def _():
            hop(0, m, b).wait_recv()

            @pl.when(q < last)
            def _():
                hop(0, m, b).start()

            pair(m, b).start()

            @pl.when(jnp.logical_and(m == q - 1, b == CHUNKS - 1))
            def _():
                rest()

        @pl.when(m > q)
        def _():
            for x in range(CHUNKS // 2):
                k = b * (CHUNKS // 2) + x
                hop(1, m, k).wait_recv()

                @pl.when(q > 0)
                def _():
                    hop(1, m, k).start()

                pair(m, k).start()

    def rest():
        for x in range(CHUNKS):

            @pl.when(jnp.logical_and(q < last, jnp.logical_and(q > 0, x >= head_start(q))))
            def _():
                hop(0, q, x).start()

    def op_product(m, b):
        other, h = lax.div(b, 2), lax.rem(b, 2)
        at = side(h)

        @pl.when(other == 1)
        def _():
            block = blocks.at[2 * m + 1 - core, :, at]
            settle(block, pair_s.at[0], pair_r.at[m, h]).wait_recv()

        j = 2 * m + core + other - 2 * core * other
        real_in, imag_in = blocks[j, 0, at, :], blocks[j, 1, at, :]
        real = mm(real_in, hist[0], NN) - mm(imag_in, hist[1], NN)
        imag = mm(real_in, hist[1], NN) + mm(imag_in, hist[0], NN)
        own_at = pl.ds(pl.multiple_of(j * height + h * half, half), half)
        for r in range(rows):

            @pl.when(row == r)
            def _():
                mine, near_x, near_y, far = [
                    slice(x * share, (x + 1) * share) for x in (r, r ^ 1, r ^ 2, r ^ 3)
                ]
                parts[j, 0, 0, at, :] = real[:, near_x].astype(bf16)
                parts[j, 0, 1, at, :] = real[:, far].astype(bf16)
                parts[j, 1, 0, at, :] = imag[:, near_y].astype(bf16)
                parts[j, 1, 1, at, :] = imag[:, far].astype(bf16)
                keep[j, 0, at, :] = real[:, near_y]
                keep[j, 1, at, :] = imag[:, near_x]
                own[0, own_at, :] = real[:, mine]
                own[1, own_at, :] = imag[:, mine]

        for k in (0, 1):
            send_parts(j, h, k).start()

    def op_join(m, b):
        other, h = lax.div(b, 2), lax.rem(b, 2)
        at = side(h)
        j = 2 * m + core + other - 2 * core * other
        for k in (0, 1):
            send_parts(j, h, k).wait_recv()
            value = keep[j, k, at, :] + first[j, k, 1, at, :].astype(jnp.float32)
            sums[j, k, at, :] = value.astype(bf16)
        for k in (0, 1):
            send_joined(j, h, k).start()

    def op_solve(j):
        at = span(j)
        for p in (0, 1):
            for h in (0, 1):
                send_joined(j, h, p).wait_recv()
            others = first[j, p, 0].astype(jnp.float32) + joined[j, p].astype(jnp.float32)
            own[p, at, :] = TIME_STEP * (own[p, at, :] + others)
        own[2, at, :] = own[0, at, :] + own[1, at, :]

        @pl.when(lax.rem(j, 2) == 1)
        def _():
            update(new, own, 0, j * times, times, j - 1)

        update(new, own, 0, j * times, times, j)

        def sigma(i, c):
            rows_at = slab(j * times + i)
            real, imag = new[0, rows_at, :], new[1, rows_at, :]
            near[0, rows_at, :] = real.astype(bf16)
            near[1, rows_at, :] = imag.astype(bf16)
            factor = weight[...] * (real * real + imag * imag)
            sigma_real = (real * factor).astype(bf16).astype(jnp.float32)
            sigma_imag = (imag * factor).astype(bf16).astype(jnp.float32)
            source[0, rows_at, :] = sigma_real
            source[1, rows_at, :] = sigma_imag
            source[2, rows_at, :] = sigma_real + sigma_imag
            return c

        lax.fori_loop(0, times, sigma, 0)

        @pl.when(lax.rem(j, 2) == 1)
        def _():
            update(tau, source, 1, j * times, times, j - 1)

        update(tau, source, 1, j * times, times, j)
        for p in (0, 1):
            taus[row, p, at, :] = (TIME_STEP * tau[p, at, :]).astype(bf16)
        for k in (0, 1):
            send_tau(j, k).start()

    def op_update(m, later_m):
        def both(half, c):
            update(new, own, 0, 2 * times * later_m, 2 * times, 2 * m + half)
            update(tau, source, 1, 2 * times * later_m, 2 * times, 2 * m + half)
            return c

        lax.fori_loop(0, 2, both, 0)

    def op_spread_tau(j):
        for k in (0, 1):
            send_tau(j, k).wait_recv()
        for k in (0, 1):
            relay_tau(j, k).start()

    def second(j):
        for k in (0, 1):
            relay_tau(j, k).wait_recv()
        at = span(j)
        real_in = jnp.concatenate([taus[r, 0, at, :] for r in range(rows)], axis=1)
        imag_in = jnp.concatenate([taus[r, 1, at, :] for r in range(rows)], axis=1)
        real = -mm(real_in, hist[0], NT) - mm(imag_in, hist[1], NT)
        imag = mm(real_in, hist[1], NT) - mm(imag_in, hist[0], NT)
        return real, imag

    def held_at(d):
        return d - jnp.where(d > q, 1, 0)

    def op_second(d, keep):
        pair_sums = second(2 * d + core + (1 - keep) * (1 - 2 * core))

        @pl.when(keep == 0)
        def _():
            for p in (0, 1):
                give[d, p] = pair_sums[p].astype(bf16)
            swap(d).start()

        @pl.when(keep == 1)
        def _():
            swap(d).wait_recv()
            begins = jnp.logical_or(
                jnp.logical_and(d < q, q == last), jnp.logical_and(d > q, q == 0)
            )

            @pl.when(d == q)
            def _():
                for p in (0, 1):
                    later[p] = pair_sums[p] + take[d, p].astype(jnp.float32)

            @pl.when(begins)
            def _():
                for p in (0, 1):
                    value = pair_sums[p] + take[d, p].astype(jnp.float32)
                    stage[d, p] = value.astype(bf16)
                for k in range(LINKS):
                    chain_on(d, k)

            @pl.when(jnp.logical_and(d != q, jnp.logical_not(begins)))
            def _():
                for p in (0, 1):
                    held[held_at(d), p] = pair_sums[p] + take[d, p].astype(jnp.float32)

    def op_chain(d, b):
        ends, way, k = lax.div(b, 2 * LINKS), lax.rem(lax.div(b, LINKS), 2), lax.rem(b, LINKS)
        at = link(k)
        slot = jnp.where(way == 1, lines, d)
        pltpu.make_async_remote_copy(
            src_ref=stage.at[d, :, at],
            dst_ref=land.at[slot, :, at],
            send_sem=chain_s.at[0],
            recv_sem=chain_r.at[slot, k],
            device_id=(row, 2 * q + 1 - core),
            device_id_type=MESH,
        ).wait_recv()

        @pl.when(d == q)
        def _():
            for p in (0, 1):
                later[p, at, :] += land[slot, p, at, :].astype(jnp.float32)

            @pl.when(ends == 1)
            def _():
                pltpu.make_async_copy(
                    later.at[:, at], later_out.at[:, at], local.at[lines]
                ).start()

        @pl.when(d != q)
        def _():
            for p in (0, 1):
                value = held[held_at(d), p, at, :] + land[slot, p, at, :].astype(jnp.float32)
                stage[d, p, at, :] = value.astype(bf16)
            chain_on(d, k)

    def op_send_near(m):
        own_near(m).start()
        for k in (0, 1):
            send_near(m, k).start()

    def op_relay_near(m):
        for k in (0, 1):
            send_near(m, k).wait_recv()
        for k in (0, 1):
            relay_near(m, k).start()

    load_hist = pltpu.make_async_copy(history, hist, local.at[lines])
    load_strip = pltpu.make_async_copy(strip, later, local.at[lines + 1])
    load_dyson = pltpu.make_async_copy(inverse, dyson, local.at[lines + 2])
    load_strip.start()
    load_hist.start()
    load_dyson.start()
    entry_barrier(row, q, core, lines, rows, False)
    place_row = lax.broadcasted_iota(jnp.int32, (orbitals, share), 0)
    place_col = lax.rem(lax.broadcasted_iota(jnp.int32, (orbitals, share), 1), orbitals)
    down = jnp.zeros((orbitals, share), jnp.float32)
    along = jnp.zeros((orbitals, share), jnp.float32)
    for a in range(orbitals):
        down = jnp.where(place_row == a, coupling[a], down)
        along = jnp.where(place_col == a, coupling[a], along)
    weight[...] = -(down * along)
    load_strip.wait()

    def fill(i, c):
        at = slab(i)
        scale = jnp.concatenate([weight[...]] * (depth // share), axis=1)
        real, imag = later[0, at, :], later[1, at, :]
        factor = scale * (real * real + imag * imag)
        blocks[col, 0, at, :] = (real * factor).astype(bf16)
        blocks[col, 1, at, :] = (imag * factor).astype(bf16)
        return c

    lax.fori_loop(0, times, fill, 0)
    entry_barrier(row, q, core, lines, rows, True)

    for x in range(CHUNKS):

        @pl.when(jnp.logical_and(q < last, jnp.logical_or(q == 0, x < head_start(q))))
        def _():
            hop(0, q, x).start()

    for x in range(CHUNKS):

        @pl.when(q > 0)
        def _():
            hop(1, q, x).start()

    for x in range(CHUNKS):
        pair(q, x).start()

    def clear(n, c):
        for p in (0, 1):
            new[p, slab(n), :] = jnp.zeros((orbitals, share), jnp.float32)
            tau[p, slab(n), :] = jnp.zeros((orbitals, share), jnp.float32)
        return c

    lax.fori_loop(0, total, clear, 0)
    load_hist.wait()
    load_dyson.wait()

    words = []
    for w in range(count // 4):
        word = jnp.int32(packed[last][w])
        for x in range(last):
            word = jnp.where(q == x, jnp.int32(packed[x][w]), word)
        words.append(word)

    def step(i, c):
        which, place = lax.div(i, 4), lax.rem(i, 4)
        level = words
        bit = 1
        while len(level) > 1:
            odd = lax.rem(lax.div(which, bit), 2) == 1
            joined_up = [
                jnp.where(odd, level[w + 1], level[w]) for w in range(0, len(level) - 1, 2)
            ]
            level = joined_up + level[len(level) - len(level) % 2 :]
            bit *= 2
        code = lax.shift_right_logical(level[0], 8 * place) & 255

        @pl.when(code < UPDATE)
        def _():
            @pl.when(code < RELAY)
            def _():
                op_chain(lax.div(code, 16), lax.rem(code, 16))

            @pl.when(code >= RELAY)
            def _():
                op_relay(lax.div(code - RELAY, 8), lax.rem(code, 8))

        @pl.when(jnp.logical_and(code >= UPDATE, code < SOLVE))
        def _():
            a, b = lax.rem(lax.div(code, 4), 4), lax.rem(code, 4)

            @pl.when(code < PRODUCT)
            def _():
                op_update(a, b)

            @pl.when(jnp.logical_and(code >= PRODUCT, code < JOIN))
            def _():
                op_product(a, b)

            @pl.when(code >= JOIN)
            def _():
                op_join(a, b)

        @pl.when(code >= SOLVE)
        def _():
            @pl.when(code < SPREAD_TAU)
            def _():
                op_solve(code - SOLVE)

            @pl.when(jnp.logical_and(code >= SPREAD_TAU, code < SECOND))
            def _():
                op_spread_tau(code - SPREAD_TAU)

            @pl.when(jnp.logical_and(code >= SECOND, code < SEND_NEAR))
            def _():
                op_second(lax.rem(code, 4), lax.div(code - SECOND, 4))

            @pl.when(jnp.logical_and(code >= SEND_NEAR, code < RELAY_NEAR))
            def _():
                op_send_near(code - SEND_NEAR)

            @pl.when(jnp.logical_and(code >= RELAY_NEAR, code < NOTHING))
            def _():
                op_relay_near(code - RELAY_NEAR)

        return c

    lax.fori_loop(0, count, step, 0)

    def drain(m, c):
        block = blocks.at[2 * m + core]

        @pl.when(jnp.logical_and(m <= q, q < last))
        def _():
            settle(block, hop_s.at[0, m], hop_r.at[m, 0]).wait_send()

        @pl.when(jnp.logical_and(m >= q, q > 0))
        def _():
            settle(block, hop_s.at[1, m], hop_r.at[m, 0]).wait_send()

        own_near(m).wait()
        for k in (0, 1):
            relay_near(m, k).wait_recv()
        return c

    lax.fori_loop(0, lines, drain, 0)
    settle(blocks.at[pl.ds(0, lines)], pair_s.at[0], pair_r.at[0, 0]).wait_send()
    for k in (0, 1):
        settle(parts.at[:, k], sum_s.at[k], sum_r.at[0, 0, 0]).wait_send()
        settle(sums.at[:, k], sum_s.at[2 + k], sum_r.at[0, 0, 0]).wait_send()
        settle(taus.at[k], tau_s.at[k], tau_r.at[0, 0]).wait_send()
        settle(taus.at[0, k], tau_s.at[2 + k], tau_r.at[0, 0]).wait_send()
        settle(near, near_s.at[k], near_r.at[0, 0]).wait_send()
        settle(near.at[k], near_s.at[2 + k], near_r.at[0, 0]).wait_send()
    settle(give, give_s.at[0], give_r.at[0]).wait_send()
    settle(stage.at[pl.ds(0, last)], chain_s.at[0], chain_r.at[0, 0]).wait_send()
    pltpu.make_async_copy(later, later_out, local.at[lines]).wait()


VMEM = pl.BlockSpec(memory_space=pltpu.VMEM)
ANY = pl.BlockSpec(memory_space=pl.ANY)
SMEM = pl.BlockSpec(memory_space=pltpu.SMEM)
DMA = pltpu.SemaphoreType.DMA


def fused(strip, history, coupling, dyson, lines, rows):
    height, depth = strip.shape[1:]
    width = history.shape[2]
    share = width // rows
    blocks = 2 * lines
    full = blocks * height
    count, packed = step_words(lines)
    bf16, f32 = jnp.bfloat16, jnp.float32
    return pl.pallas_call(
        functools.partial(fused_kernel, lines, rows, count, packed),
        out_shape=(
            jax.ShapeDtypeStruct(strip.shape, f32),
            jax.ShapeDtypeStruct((2, full, width), bf16),
        ),
        in_specs=[ANY, ANY, SMEM, ANY],
        out_specs=(ANY, ANY),
        scratch_shapes=[
            pltpu.SMEM(dyson.shape, f32),
            pltpu.VMEM(strip.shape, f32),
            pltpu.VMEM(history.shape, bf16),
            pltpu.VMEM((coupling.shape[0], share), f32),
            pltpu.VMEM((blocks, 2, height, depth), bf16),
            pltpu.VMEM((blocks, 2, 2, height, share), bf16),
            pltpu.VMEM((blocks, 2, 2, height, share), bf16),
            pltpu.VMEM((blocks, 2, height, share), f32),
            pltpu.VMEM((blocks, 2, height, share), bf16),
            pltpu.VMEM((blocks, 2, height, share), bf16),
            pltpu.VMEM((3, full, share), f32),
            pltpu.VMEM((2, full, share), f32),
            pltpu.VMEM((2, full, share), f32),
            pltpu.VMEM((3, full, share), f32),
            pltpu.VMEM((2, full, share), bf16),
            pltpu.VMEM((rows, 2, full, share), bf16),
            pltpu.VMEM((lines, 2, height, depth), bf16),
            pltpu.VMEM((lines, 2, height, depth), bf16),
            pltpu.VMEM((lines, 2, height, depth), bf16),
            pltpu.VMEM((lines + 1, 2, height, depth), bf16),
            pltpu.VMEM((lines - 1, 2, height, depth), f32),
            DMA((2, lines)),
            DMA((lines, CHUNKS)),
            DMA((1,)),
            DMA((lines, 2)),
            DMA((4,)),
            DMA((blocks, 2, 4)),
            DMA((4,)),
            DMA((blocks, 4)),
            DMA((4,)),
            DMA((lines, 4)),
            DMA((lines + 3,)),
            DMA((1,)),
            DMA((lines,)),
            DMA((1,)),
            DMA((lines + 1, LINKS)),
        ],
        compiler_params=pltpu.CompilerParams(
            collective_id=0, has_side_effects=True, vmem_limit_bytes=63 * 1024 * 1024
        ),
        name="group_updates",
    )(strip, history, coupling, dyson)


def widen_kernel(pieces, wide, later, out, later_out, rough, fine, passing, in_s, out_s, pass_s):
    size = wide.shape[1] // pieces

    def fetch(i):
        return pltpu.make_async_copy(wide.at[:, pl.ds(i * size, size)], rough.at[i], in_s.at[i])

    def put(i):
        return pltpu.make_async_copy(fine.at[i], out.at[:, pl.ds(i * size, size)], out_s.at[i])

    take = pltpu.make_async_copy(later, passing, pass_s.at[0])
    leave = pltpu.make_async_copy(passing, later_out, pass_s.at[1])
    for i in range(pieces):
        fetch(i).start()
    take.start()
    for i in range(pieces):
        fetch(i).wait()
        fine[i] = rough[i].astype(jnp.float32)
        put(i).start()
    take.wait()
    leave.start()
    for i in range(pieces):
        put(i).wait()
    leave.wait()


def widen(wide, later):
    pieces = 8
    piece = (pieces, 2, wide.shape[1] // pieces, wide.shape[2])
    return pl.pallas_call(
        functools.partial(widen_kernel, pieces),
        out_shape=(
            jax.ShapeDtypeStruct(wide.shape, jnp.float32),
            jax.ShapeDtypeStruct(later.shape, jnp.float32),
        ),
        in_specs=[ANY, ANY],
        out_specs=(ANY, ANY),
        scratch_shapes=[
            pltpu.VMEM(piece, jnp.bfloat16),
            pltpu.VMEM(piece, jnp.float32),
            pltpu.VMEM(later.shape, jnp.float32),
            DMA((pieces,)),
            DMA((pieces,)),
            DMA((2,)),
        ],
        compiler_params=pltpu.CompilerParams(vmem_limit_bytes=60 * 1024 * 1024),
        name="widen",
    )(wide, later)


def stacked_dyson(inverse, source):
    group_len = inverse.shape[1]
    matrix = TIME_STEP * jnp.concatenate(
        [
            jnp.concatenate([inverse[0], -inverse[1]], axis=1),
            jnp.concatenate([inverse[1], inverse[0]], axis=1),
        ],
        axis=0,
    )
    flat = source.reshape(2 * group_len, -1)
    solved = jnp.dot(
        matrix, flat, precision=lax.Precision.HIGHEST, preferred_element_type=jnp.float32
    )
    return solved.reshape(source.shape)


def shards(history, start_strip, coupling, dyson_inverse):
    row_count = lax.axis_size("row")
    col_count = lax.axis_size("col")
    row_index = lax.axis_index("row")
    col_index = lax.axis_index("col")
    strip_rows = start_strip.shape[1]
    strip_cols = start_strip.shape[2]
    group_rows = strip_rows * col_count
    tile_cols = history.shape[2]
    share_cols = tile_cols // row_count
    orbitals = coupling.shape[0]
    fits = (
        row_count == 4
        and col_count // 2 in ORDERS
        and col_count % 2 == 0
        and share_cols == 128
        and share_cols % orbitals == 0
        and strip_rows % (16 * CHUNKS) == 0
        and strip_rows % (16 * LINKS) == 0
        and strip_rows % 32 == 0
        and strip_rows % orbitals == 0
        and group_rows // orbitals == dyson_inverse.shape[2]
    )
    if fits:
        later_strip, wide = fused(
            start_strip, history, coupling, dyson_inverse, col_count // 2, row_count
        )
        return widen(wide, later_strip)
    sigma_first = self_energy(
        start_strip,
        orbital_weights(coupling, col_index * strip_rows, strip_rows),
        orbital_weights(coupling, row_index * strip_cols, strip_cols),
    ).astype(jnp.bfloat16)
    partial_first = complex_product(
        lax.all_gather(sigma_first, "col", axis=1, tiled=True), history
    )
    shares = lax.psum_scatter(partial_first, "row", scatter_dimension=2, tiled=True)
    solved_part = stacked_dyson(dyson_inverse[0], shares)
    sigma_second = self_energy(
        solved_part,
        orbital_weights(coupling, 0, group_rows),
        orbital_weights(coupling, col_index * tile_cols + row_index * share_cols, share_cols),
    ).astype(jnp.bfloat16)
    solved_sigma = stacked_dyson(
        dyson_inverse[1], sigma_second.astype(jnp.float32)
    ).astype(jnp.bfloat16)
    earlier = lax.all_gather(solved_part, "row", axis=2, tiled=True)
    tau = lax.all_gather(solved_sigma, "row", axis=2, tiled=True)
    partial_second = mirror_product(tau, history)
    later_strip = lax.psum_scatter(partial_second, "col", scatter_dimension=1, tiled=True)
    return (earlier, later_strip)


def solution(mesh):
    return jax.shard_map(
        shards,
        mesh=mesh,
        in_specs=(P(None, "row", "col"), P(None, "col", "row"), P(), P()),
        out_specs=(P(None, None, "col"), P(None, "col", "row")),
        check_vma=False,
    )
```
